256 devices in a mesh: seq: 32 (over z, y), dp: 8 (over x, core).
Axes of the slice: x: 4, y: 4, z: 8, core: 2. Of those that a mesh axis runs over, the one named last changes fastest.
Arguments:
- queries: bfloat16 [8, 4096, 4096], P('dp', 'seq'), may hold values from -118 to 118
- keys: bfloat16 [8, 4096, 1024], P('dp', 'seq'), may hold values from -9 to 9
- hidden: bfloat16 [8, 4096, 4096], P('dp', 'seq'), may hold values from -6 to 6
- value_weight: bfloat16 [4096, 1024], P('dp'), may hold values from -0.09375 to 0.09375
- readout: bfloat16 [4096, 256], replicated, may hold values from -1.796875 to 1.796875
- base_logits: float32 [8, 4096, 256], P('dp', 'seq'), may hold values from -12 to 300
- labels: int32 [8, 4096], P('dp', 'seq'), may hold values from 0 to 255
- hessian: float32 [1024, 4096], P('seq', 'dp'), may hold values from 0.05 to 2
Outputs:
- estimate: float32 [1024, 4096], P('seq', 'dp')
- hessian_new: float32 [1024, 4096], P('seq', 'dp')
The draws below stay inside these ranges and needn't reach their ends.
All inputs are finite; a program needn't handle non-finite values.
Results may differ from the reference program's by a relative error of at most 0.033.
Values may be sent and summed in bfloat16 or wider, within the bound.
A program may use at most 64 MiB of HBM per device.

```python
import math
import jax
import jax.numpy as jnp
from jax import lax

D = 4096
HQ = 32
KV = 8
HD = 128
CAND = 256
LENGTH = 4096
SEQS = 8
GROUP = 4


def attention_pair(key):
    base = jax.random.fold_in(key, 17)
    first, second = jax.random.split(base, 2)
    queries = jnp.clip(1.5 * jax.random.normal(first, (SEQS, LENGTH, HQ, HD), jnp.float32), -9.0, 9.0)
    keys = jnp.clip(1.5 * jax.random.normal(second, (SEQS, LENGTH, KV, HD), jnp.float32), -9.0, 9.0)
    return (queries.reshape(SEQS, LENGTH, HQ * HD), keys.reshape(SEQS, LENGTH, KV * HD))


def draw_queries(key, part):
    return attention_pair(key)[0].astype(jnp.bfloat16)


def draw_keys(key, part):
    return attention_pair(key)[1].astype(jnp.bfloat16)


def draw_base_logits(key, part):
    base = jax.random.fold_in(key, 29)
    first = jax.random.fold_in(base, 0)
    logits = jnp.clip(2.0 * jax.random.normal(first, (SEQS, LENGTH, CAND), jnp.float32), -12.0, 12.0)
    return logits


def place_ends(result, key, low, high):
    spot = [jax.random.randint(jax.random.fold_in(key, axis), (), 0, length) for axis, length in enumerate(result.shape)]
    longest = result.shape.index(max(result.shape))
    beside = spot[:longest] + [(spot[longest] + 1) % result.shape[longest]] + spot[longest + 1:]
    return result.at[tuple(spot)].set(low).at[tuple(beside)].set(high)


def steps_of(stream_key, dims, cuts, smallest, high):
    gain, own = 1.0, jax.random.fold_in(stream_key, 6)
    for dim, parts in cuts:
        steps = jnp.exp(jax.random.uniform(jax.random.fold_in(own, dim), (parts,), jnp.float32, smallest / len(cuts), high / len(cuts)))
        gain = gain * jnp.repeat(steps, dims[dim] // parts).reshape([-1 if axis == dim else 1 for axis in range(len(dims))])
    return gain


def bell_draw(rng, dims, scale, reach, cuts=(), dtype=jnp.bfloat16):
    values = scale * jax.random.normal(rng, dims, jnp.float32)
    if cuts:
        values = values * steps_of(rng, dims, cuts, -0.22, 0.18)
    return jnp.clip(values, -reach, reach).astype(dtype)


def setup_inputs(seed: int = 0) -> dict:
    seeds = jax.random.split(jax.random.key(seed), 9)
    queries = draw_queries(jax.random.fold_in(seeds[8], 71), 0)
    keys = draw_keys(jax.random.fold_in(seeds[8], 71), 0)
    hidden = bell_draw(seeds[2], (SEQS, LENGTH, D), 1.0, 6.0, ((0, 8), (1, 32)))
    value_weight = bell_draw(seeds[3], (D, KV * HD), D ** -0.5, 0.09375, ((0, 8),))
    readout = bell_draw(seeds[4], (HQ * HD, CAND), 0.3, 1.796875)
    base_logits = draw_base_logits(jax.random.fold_in(seeds[8], 71), 0)
    labels = place_ends(jax.random.randint(seeds[6], (SEQS, LENGTH), 0, CAND), jax.random.fold_in(seeds[6], 1), 0, CAND - 1).astype(jnp.int32)
    hessian = jnp.clip(jnp.exp(math.log(2.0) - 3.6888794 * jax.random.uniform(seeds[7], (KV * HD, D), jnp.float32) ** steps_of(seeds[7], (KV * HD, D), ((0, 32), (1, 8)), -0.2, 0.2)), 0.05, 2.0)
    return dict(queries=queries, keys=keys, hidden=hidden, value_weight=value_weight, readout=readout, base_logits=base_logits, labels=labels, hessian=hessian)


big_negative = -1.0e30
beta_two = 0.99


def block_scores(q_block, k_block, row_start, col_start, scale):
    scores = jnp.einsum("hqd,hkd->hqk", q_block.astype(jnp.float32), k_block.astype(jnp.float32), precision=lax.Precision.HIGHEST) * scale
    rows_pos = row_start + lax.broadcasted_iota(jnp.int32, scores.shape, 1)
    cols_pos = col_start + lax.broadcasted_iota(jnp.int32, scores.shape, 2)
    return jnp.where(cols_pos <= rows_pos, scores, big_negative)


def row_statistics(queries, keys, width, scale):
    heads, length, _ = queries.shape
    blocks = length // width

    def outer(i, state):
        i = jnp.asarray(i).astype(jnp.int32)
        peak_all, total_all = state
        q_block = lax.dynamic_slice_in_dim(queries, i * width, width, 1)

        def inner(j, carry):
            j = jnp.asarray(j).astype(jnp.int32)
            peak, total = carry
            k_block = lax.dynamic_slice_in_dim(keys, j * width, width, 1)
            scores = block_scores(q_block, k_block, i * width, j * width, scale)
            fresh = jnp.maximum(peak, jnp.max(scores, axis=2))
            total = total * jnp.exp(peak - fresh) + jnp.sum(jnp.exp(scores - fresh[:, :, None]), axis=2)
            return fresh, total

        starting = (jnp.full((heads, width), big_negative, jnp.float32), jnp.zeros((heads, width), jnp.float32))
        peak, total = lax.fori_loop(0, i + 1, inner, starting)
        peak_all = lax.dynamic_update_slice_in_dim(peak_all, peak, i * width, 1)
        total_all = lax.dynamic_update_slice_in_dim(total_all, total, i * width, 1)
        return peak_all, total_all

    starting = (jnp.zeros((heads, length), jnp.float32), jnp.zeros((heads, length), jnp.float32))
    return lax.fori_loop(0, blocks, outer, starting)


def attend(queries, keys, values, peak, total, width, scale):
    heads, length, dim = queries.shape
    blocks = length // width

    def outer(i, output):
        i = jnp.asarray(i).astype(jnp.int32)
        q_block = lax.dynamic_slice_in_dim(queries, i * width, width, 1)
        peak_block = lax.dynamic_slice_in_dim(peak, i * width, width, 1)
        total_block = lax.dynamic_slice_in_dim(total, i * width, width, 1)

        def inner(j, running):
            j = jnp.asarray(j).astype(jnp.int32)
            k_block = lax.dynamic_slice_in_dim(keys, j * width, width, 1)
            v_block = lax.dynamic_slice_in_dim(values, j * width, width, 1)
            scores = block_scores(q_block, k_block, i * width, j * width, scale)
            weights = (jnp.exp(scores - peak_block[:, :, None]) / total_block[:, :, None]).astype(jnp.bfloat16)
            return running + jnp.einsum("hqk,hkd->hqd", weights.astype(jnp.float32), v_block.astype(jnp.float32), precision=lax.Precision.HIGHEST)

        running = lax.fori_loop(0, i + 1, inner, jnp.zeros((heads, width, dim), jnp.float32))
        return lax.dynamic_update_slice_in_dim(output, running.astype(jnp.bfloat16), i * width, 1)

    return lax.fori_loop(0, blocks, outer, jnp.zeros((heads, length, dim), jnp.bfloat16))


def value_grads(queries, keys, d_out, peak, total, width, scale):
    heads, length, dim = queries.shape
    blocks = length // width

    def outer(j, output):
        j = jnp.asarray(j).astype(jnp.int32)
        k_block = lax.dynamic_slice_in_dim(keys, j * width, width, 1)

        def inner(i, running):
            i = jnp.asarray(i).astype(jnp.int32)
            q_block = lax.dynamic_slice_in_dim(queries, i * width, width, 1)
            d_block = lax.dynamic_slice_in_dim(d_out, i * width, width, 1)
            peak_block = lax.dynamic_slice_in_dim(peak, i * width, width, 1)
            total_block = lax.dynamic_slice_in_dim(total, i * width, width, 1)
            scores = block_scores(q_block, k_block, i * width, j * width, scale)
            weights = (jnp.exp(scores - peak_block[:, :, None]) / total_block[:, :, None]).astype(jnp.bfloat16)
            return running + jnp.einsum("hqk,hqd->hkd", weights.astype(jnp.float32), d_block.astype(jnp.float32), precision=lax.Precision.HIGHEST)

        running = lax.fori_loop(j, blocks, inner, jnp.zeros((heads, width, dim), jnp.float32))
        return lax.dynamic_update_slice_in_dim(output, running.astype(jnp.bfloat16), j * width, 1)

    return lax.fori_loop(0, blocks, outer, jnp.zeros((heads, length, dim), jnp.bfloat16))


def reference(queries, keys, hidden, value_weight, readout, base_logits, labels, hessian):
    width = min(512, LENGTH)
    scale = 1.0 / (HD ** 0.5)
    flat_hidden = hidden.reshape(SEQS * LENGTH, D)
    values = jnp.dot(flat_hidden, value_weight, preferred_element_type=jnp.float32).astype(jnp.bfloat16)
    values = values.reshape(SEQS, LENGTH, KV * HD)

    def spread_heads(array, count, repeat):
        split = array.reshape(LENGTH, count, HD).transpose(1, 0, 2)
        return jnp.repeat(split, repeat, axis=0)

    def forward_one(operands):
        query_seq, key_seq, value_seq = operands
        q_heads = spread_heads(query_seq, HQ, 1)
        k_heads = spread_heads(key_seq, KV, GROUP)
        v_heads = spread_heads(value_seq, KV, GROUP)
        peak, total = row_statistics(q_heads, k_heads, width, scale)
        output = attend(q_heads, k_heads, v_heads, peak, total, width, scale)
        return output.transpose(1, 0, 2).reshape(LENGTH, HQ * HD), peak, total

    attended, peak, total = lax.map(forward_one, (queries, keys, values))
    logits = base_logits.reshape(SEQS * LENGTH, CAND) + jnp.dot(attended.reshape(SEQS * LENGTH, HQ * HD), readout, preferred_element_type=jnp.float32)
    softmax_rows = jax.nn.softmax(logits, axis=1)
    chosen = labels.reshape(SEQS * LENGTH, 1) == lax.broadcasted_iota(jnp.int32, logits.shape, 1)
    d_logits = (softmax_rows - chosen.astype(jnp.float32)).astype(jnp.bfloat16)
    d_attended = jnp.dot(d_logits, readout.T, preferred_element_type=jnp.float32).astype(jnp.bfloat16)
    d_attended = d_attended.reshape(SEQS, LENGTH, HQ * HD)

    def backward_one(operands):
        query_seq, key_seq, d_seq, peak_seq, total_seq = operands
        q_heads = spread_heads(query_seq, HQ, 1)
        k_heads = spread_heads(key_seq, KV, GROUP)
        d_heads = spread_heads(d_seq, HQ, 1)
        d_head = value_grads(q_heads, k_heads, d_heads, peak_seq, total_seq, width, scale)
        summed = d_head.astype(jnp.float32).reshape(KV, GROUP, LENGTH, HD).sum(axis=1).astype(jnp.bfloat16)
        return summed.transpose(1, 0, 2).reshape(LENGTH, KV * HD)

    d_values = lax.map(backward_one, (queries, keys, d_attended, peak, total))
    grad_sum = jnp.dot(d_values.reshape(SEQS * LENGTH, KV * HD).T, flat_hidden, preferred_element_type=jnp.float32)
    estimate = grad_sum * grad_sum / (SEQS * LENGTH)
    return estimate, beta_two * hessian + (1.0 - beta_two) * estimate
```

```python
import functools
import math
import types

import jax
import jax.numpy as jnp
from jax import lax
from jax.experimental import pallas as pl
from jax.experimental.pallas import tpu as pltpu
from jax.sharding import PartitionSpec as P

HD = 128
TOK = 128
SMALL = -1.0e30
beta_two = 0.99
MESH = pl.DeviceIdType.MESH
F32 = jnp.float32
BF16 = jnp.bfloat16
VMEM = pl.BlockSpec(memory_space=pltpu.VMEM)
ANY = pl.BlockSpec(memory_space=pl.ANY)


def sizes_of(seq, dp):
    n = types.SimpleNamespace(S=seq, P=dp, C=2, X=dp // 2)
    n.Y = 4 if seq == 32 else 2
    n.Z = seq // n.Y
    return n


def place():
    return lax.axis_index("seq"), lax.axis_index("dp")


def rem(a, b):
    return lax.rem(a, jnp.int32(b))


def loop(low, high, step):
    def body(i, carry):
        step(i)
        return carry

    lax.fori_loop(low, high, body, 0)


def aligned(start, size):
    return pl.ds(pl.multiple_of(start, size), size)


def send(src, dst, send_sem, recv_sem, seq, dp):
    return pltpu.make_async_remote_copy(
        src_ref=src,
        dst_ref=dst,
        send_sem=send_sem,
        recv_sem=recv_sem,
        device_id=(seq, dp),
        device_id_type=MESH,
    )


def greet(peers):
    barrier = pltpu.get_barrier_semaphore()
    count = 0
    for low, high, where in peers:

        def one(d, where=where):
            seq, dp = where(d)
            pl.semaphore_signal(barrier, inc=1, device_id=(seq, dp), device_id_type=MESH)

        loop(low, high, one)
        count += high - low
    pl.semaphore_wait(barrier, count)


def front_kernel(
    n,
    hidden,
    queries,
    keys,
    weight,
    cols,
    qz,
    kz,
    vz,
    part,
    pair,
    both,
    xin,
    val,
    loc,
    hs,
    hr,
    qs,
    qr,
    ks,
    kr,
    kys,
    kyr,
    cs,
    cr,
    xs,
    xr,
    vs,
    vr,
    vys,
    vyr,
):
    seq, dp = place()
    Z, Y, X, C, PP = n.Z, n.Y, n.X, n.C, n.P
    z, y = seq // Y, rem(seq, Y)
    x, c = dp // C, rem(dp, C)
    feat = hidden.shape[1] // PP
    qw = queries.shape[1] // Z

    def zpeer(d):
        return rem(z + d, Z) * Y + y, dp

    def ypeer(e):
        return z * Y + rem(y + e, Y), dp

    def ppeer(d):
        return seq, rem(dp + d, PP)

    greet(((1, Z, zpeer), (1, Y, ypeer), (1, PP, ppeer)))

    def slot_of(p):
        return rem(p, C) * X + p // C

    def lanes(ref, i, width):
        return ref.at[:, aligned(i * width, width)]

    def k_send(d):
        to = rem(z + d, Z)
        return send(lanes(keys, to, HD), kz.at[seq], ks.at[d], kr.at[d], to * Y + y, dp)

    def h_send(d):
        to = rem(dp + d, PP)
        return send(lanes(hidden, to, feat), cols.at[slot_of(dp)], hs.at[d], hr.at[d], seq, to)

    def q_send(d):
        to = rem(z + d, Z)
        return send(lanes(queries, to, qw), qz.at[z], qs.at[d], qr.at[d], to * Y + y, dp)

    loop(1, Z, lambda d: k_send(d).start())
    loop(1, PP, lambda d: h_send(d).start())
    loop(1, Z, lambda d: q_send(d).start())
    own_k = pltpu.make_async_copy(lanes(keys, z, HD), kz.at[seq], loc.at[0])
    own_h = pltpu.make_async_copy(lanes(hidden, dp, feat), cols.at[slot_of(dp)], loc.at[1])
    own_q = pltpu.make_async_copy(lanes(queries, z, qw), qz.at[z], loc.at[2])
    own_k.start()
    own_h.start()
    own_q.start()

    def forward(ref, first, d, e, ssem, rsem):
        at = rem(z - d + Z, Z) * Y + y
        src = first if first is not None else ref.at[at]
        to = rem(y + e, Y)
        return send(src, ref.at[at], ssem.at[d, e], rsem.at[d, e], z * Y + to, dp)

    def forward_all(ref, mine, sent, ssem, rsem):
        loop(1, Y, lambda e: forward(ref, mine, 0, e, ssem, rsem).start())

        def step(d):
            sent(d).wait_recv()
            loop(1, Y, lambda e: forward(ref, None, d, e, ssem, rsem).start())

        loop(1, Z, step)

    def forward_done(ref, mine, ssem, rsem):
        loop(1, Y, lambda e: forward(ref, mine, 0, e, ssem, rsem).wait())
        loop(1, Z, lambda d: loop(1, Y, lambda e: forward(ref, None, d, e, ssem, rsem).wait()))

    forward_all(kz, lanes(keys, z, HD), k_send, kys, kyr)

    own_h.wait()
    loop(1, PP, lambda d: h_send(d).wait_recv())
    rows = X * TOK
    width = min(512, part.shape[1])

    def product(half):
        block = cols[pl.ds(half * X, X)].reshape(rows, feat)
        for w in range(0, part.shape[1], width):
            part[pl.ds(pl.multiple_of(half * rows, rows), rows), w : w + width] = jnp.dot(
                block, weight[:, w : w + width], preferred_element_type=F32
            ).astype(BF16)

    other = 1 - c

    def c_send(i):
        row = aligned((other * X + i) * TOK, TOK)
        return send(part.at[row], pair.at[i], cs.at[i], cr.at[i], seq, x * C + other)

    product(other)
    loop(0, X, lambda i: c_send(i).start())
    product(c)

    def x_send(d):
        to = rem(x + d, X)
        return send(both.at[to], xin.at[d], xs.at[d], xr.at[d], seq, to * C + c)

    def join(d):
        to = rem(x + d, X)
        c_send(to).wait_recv()
        mine = part[aligned((c * X + to) * TOK, TOK)].astype(F32)
        both[to] = (mine + pair[to].astype(F32)).astype(BF16)

    def join_send(d):
        join(d)
        x_send(d).start()

    loop(1, X, join_send)
    join(jnp.int32(X))
    total = both[x].astype(F32)
    for d in range(1, X):
        x_send(d).wait_recv()
        total = total + xin[d].astype(F32)
    val[...] = total.astype(BF16)

    def v_send(d):
        to = rem(z + d, Z)
        return send(lanes(val, to, HD), vz.at[seq], vs.at[d], vr.at[d], to * Y + y, dp)

    own_v = pltpu.make_async_copy(lanes(val, z, HD), vz.at[seq], loc.at[3])
    loop(1, Z, lambda d: v_send(d).start())
    own_v.start()
    forward_all(vz, lanes(val, z, HD), v_send, vys, vyr)

    own_k.wait()
    own_q.wait()
    own_v.wait()
    loop(1, Z, lambda d: q_send(d).wait())
    loop(1, Z, lambda d: k_send(d).wait_send())
    loop(1, Z, lambda d: v_send(d).wait_send())
    loop(1, PP, lambda d: h_send(d).wait_send())
    loop(0, X, lambda i: c_send(i).wait_send())
    loop(1, X, lambda d: x_send(d).wait_send())
    forward_done(kz, lanes(keys, z, HD), kys, kyr)
    forward_done(vz, lanes(val, z, HD), vys, vyr)


def front(n, hidden, queries, keys, weight):
    feat = hidden.shape[1] // n.P
    qw = queries.shape[1] // n.Z
    kv = keys.shape[1]
    dma = pltpu.SemaphoreType.DMA
    shape = jax.ShapeDtypeStruct
    return pl.pallas_call(
        functools.partial(front_kernel, n),
        out_shape=(
            shape((n.P, TOK, feat), BF16),
            shape((n.Z, TOK, qw), BF16),
            shape((n.S, TOK, HD), BF16),
            shape((n.S, TOK, HD), BF16),
        ),
        in_specs=[ANY, ANY, ANY, VMEM],
        out_specs=(VMEM, VMEM, VMEM, VMEM),
        scratch_shapes=[
            pltpu.VMEM((n.P * TOK, kv), BF16),
            pltpu.VMEM((n.X, TOK, kv), BF16),
            pltpu.VMEM((n.X, TOK, kv), BF16),
            pltpu.VMEM((n.X, TOK, kv), BF16),
            pltpu.VMEM((TOK, kv), BF16),
            dma((4,)),
            dma((n.P,)),
            dma((n.P,)),
            dma((n.Z,)),
            dma((n.Z,)),
            dma((n.Z,)),
            dma((n.Z,)),
            dma((n.Z, n.Y)),
            dma((n.Z, n.Y)),
            dma((n.X,)),
            dma((n.X,)),
            dma((n.X,)),
            dma((n.X,)),
            dma((n.Z,)),
            dma((n.Z,)),
            dma((n.Z, n.Y)),
            dma((n.Z, n.Y)),
        ],
        compiler_params=pltpu.CompilerParams(collective_id=0, has_side_effects=True),
        name="front",
    )(hidden, queries, keys, weight)


def contract(a, b, da, db):
    return lax.dot_general(a, b, (((da,), (db,)), ((), ())), preferred_element_type=F32)


def attend_kernel(n, group, qz, k, v, readout, logits, kept, inverse, raw, vt, out):
    y = rem(lax.axis_index("seq"), n.Y)
    chunk = n.Y * TOK
    wide = group * TOK
    factor = math.log2(math.e) / math.sqrt(HD)

    def turn(j):
        vt[j] = v[aligned(j * chunk, chunk), :].astype(F32).T.astype(BF16)

    loop(0, n.Z, turn)

    def fold(a, op):
        return op(a.reshape(chunk // 8, 8, wide), axis=0)

    def block(t):
        q_block = qz[t]
        q_rows = jnp.concatenate([q_block[:, h * HD : (h + 1) * HD] for h in range(group)], axis=0)
        base = t * (t + 1) // 2

        def scores(j):
            return contract(k[aligned(j * chunk, chunk), :], q_rows, 1, 1)

        def first(j, peak):
            s = scores(j)
            raw[aligned(j * chunk, chunk), :] = s
            return jnp.maximum(peak, fold(s, jnp.max))

        s = scores(t)
        key_at = lax.broadcasted_iota(jnp.int32, (chunk, wide), 0)
        query_at = lax.broadcasted_iota(jnp.int32, (chunk, wide), 1)
        seen = key_at <= (query_at & (TOK - 1)) + y * TOK
        s = jnp.where(seen, s, SMALL)
        raw[aligned(t * chunk, chunk), :] = s
        peak = lax.fori_loop(0, t, first, fold(s, jnp.max))
        peak = jnp.max(peak, axis=0, keepdims=True)
        out[...] = jnp.zeros_like(out)

        def second(j, total):
            e = jnp.exp2((raw[aligned(j * chunk, chunk), :] - peak) * factor)
            rounded = e.astype(BF16)
            kept[base + j] = rounded
            out[...] += jnp.dot(vt[j], rounded, preferred_element_type=F32)
            return total + fold(e, jnp.sum)

        total = lax.fori_loop(0, t + 1, second, jnp.zeros((8, wide), F32))
        scale = 1.0 / jnp.sum(total, axis=0, keepdims=True)
        inverse[t] = jnp.broadcast_to(scale, (8, wide))
        mixed = (out[...] * scale).astype(BF16)
        share = jnp.zeros((TOK, readout.shape[1]), F32)
        for h in range(group):
            at = slice(h * HD, (h + 1) * HD)
            share = share + contract(mixed[:, at], readout[at, :], 0, 0)
        logits[t] = share.astype(BF16)

    loop(0, n.Z, block)


def attend(n, qz, k, v, readout):
    group = qz.shape[2] // HD
    chunk = n.Y * TOK
    wide = group * TOK
    shape = jax.ShapeDtypeStruct
    return pl.pallas_call(
        functools.partial(attend_kernel, n, group),
        out_shape=(
            shape((n.Z, TOK, readout.shape[1]), BF16),
            shape((n.Z * (n.Z + 1) // 2, chunk, wide), BF16),
            shape((n.Z, 8, wide), F32),
        ),
        in_specs=[VMEM] * 4,
        out_specs=(VMEM, VMEM, VMEM),
        scratch_shapes=[
            pltpu.VMEM((n.Z * chunk, wide), F32),
            pltpu.VMEM((n.Z, HD, chunk), BF16),
            pltpu.VMEM((HD, wide), F32),
        ],
        name="attend",
    )(qz, k, v, readout)


def logit_kernel(n, share, base, labels, slopes, arrived, ss, sr, ds, dr):
    seq, dp = place()
    Z, Y = n.Z, n.Y
    z, y = seq // Y, rem(seq, Y)

    def zpeer(d):
        return rem(z + d, Z) * Y + y, dp

    greet(((1, Z, zpeer),))

    def l_send(d):
        to = rem(z + d, Z)
        return send(share.at[to], arrived.at[d], ss.at[d], sr.at[d], to * Y + y, dp)

    loop(1, Z, lambda d: l_send(d).start())
    total = base[...] + share[z].astype(F32)
    for d in range(1, Z):
        l_send(d).wait_recv()
        total = total + arrived[d].astype(F32)
    peak = jnp.max(total, axis=1, keepdims=True)
    e = jnp.exp(total - peak)
    soft = e / jnp.sum(e, axis=1, keepdims=True)
    chosen = labels[...] == lax.broadcasted_iota(jnp.int32, total.shape, 1)
    slopes[z] = (soft - jnp.where(chosen, 1.0, 0.0)).astype(BF16)

    def d_send(d):
        return send(slopes.at[z], slopes.at[z], ds.at[d], dr.at[d], *zpeer(d))

    loop(1, Z, lambda d: d_send(d).start())
    loop(1, Z, lambda d: l_send(d).wait_send())
    loop(1, Z, lambda d: d_send(d).wait())


def logit_slopes(n, share, base, labels):
    dma = pltpu.SemaphoreType.DMA
    return pl.pallas_call(
        functools.partial(logit_kernel, n),
        out_shape=jax.ShapeDtypeStruct(share.shape, BF16),
        in_specs=[VMEM] * 3,
        out_specs=VMEM,
        scratch_shapes=[pltpu.VMEM(share.shape, BF16)] + [dma((n.Z,))] * 4,
        compiler_params=pltpu.CompilerParams(collective_id=1, has_side_effects=True),
        name="logits",
    )(share, base, labels)


def grads_kernel(n, group, slopes, readout, kept, inverse, grads, total):
    chunk = n.Y * TOK
    total[...] = jnp.zeros_like(total)

    def block(t):
        base = t * (t + 1) // 2
        slope = slopes[t]
        parts = []
        for h in range(group):
            at = slice(h * HD, (h + 1) * HD)
            d = contract(slope, readout[at, :], 1, 1)
            column = inverse[t][:, at].T[:, :1]
            parts.append((d * column).astype(BF16))
        d_rows = jnp.concatenate(parts, axis=0)

        def inner(j):
            total[aligned(j * chunk, chunk), :] += jnp.dot(
                kept[base + j], d_rows, preferred_element_type=F32
            )

        loop(0, t + 1, inner)

    loop(0, n.Z, block)

    def put(j):
        for i in range(n.Y):
            grads[i, j] = total[aligned(j * chunk + i * TOK, TOK), :].astype(BF16)

    loop(0, n.Z, put)


def value_grads(n, slopes, readout, kept, inverse):
    group = readout.shape[0] // HD
    return pl.pallas_call(
        functools.partial(grads_kernel, n, group),
        out_shape=jax.ShapeDtypeStruct((n.Y, n.Z, TOK, HD), BF16),
        in_specs=[VMEM] * 4,
        out_specs=VMEM,
        scratch_shapes=[pltpu.VMEM((n.S * TOK, HD), F32)],
        name="value_grads",
    )(slopes, readout, kept, inverse)


def last_kernel(
    n,
    grads,
    cols,
    hessian,
    estimate,
    updated,
    ya,
    dz,
    dv,
    gp,
    gy,
    gz,
    gr,
    y1s,
    y1r,
    z1s,
    z1r,
    xs,
    xr,
    cs,
    cr,
    y2s,
    y2r,
    z2s,
    z2r,
    loc,
):
    seq, dp = place()
    Z, Y, X, C, PP = n.Z, n.Y, n.X, n.C, n.P
    z, y = seq // Y, rem(seq, Y)
    x, c = dp // C, rem(dp, C)
    slot = c * X + x
    rows, feat = hessian.shape

    def zpeer(d):
        return rem(z + d, Z) * Y + y, dp

    def ypeer(e):
        return z * Y + rem(y + e, Y), dp

    def xpeer(d):
        return seq, rem(x + d, X) * C + c

    sibling = x * C + 1 - c
    greet(((1, Z, zpeer), (1, Y, ypeer), (1, X, xpeer), (0, 1, lambda d: (seq, sibling))))

    def y1(e):
        return send(grads.at[rem(y + e, Y)], ya.at[e], y1s.at[e], y1r.at[e], *ypeer(e))

    loop(1, Y, lambda e: y1(e).start())
    loop(1, Y, lambda e: y1(e).wait_recv())

    def z1(d):
        to = rem(z + d, Z)
        dst = dv.at[slot, :, aligned(z * HD, HD)]
        return send(dz.at[to], dst, z1s.at[d], z1r.at[d], to * Y + y, dp)

    def add(to):
        block = grads[y, to].astype(F32)
        for e in range(1, Y):
            block = block + ya[e, to].astype(F32)
        dz[to] = block.astype(BF16)

    def add_send(d):
        add(rem(z + d, Z))
        z1(d).start()

    loop(1, Z, add_send)
    add(z)
    own = pltpu.make_async_copy(dz.at[z], dv.at[slot, :, aligned(z * HD, HD)], loc.at[0])
    own.start()
    own.wait()
    loop(1, Z, lambda d: z1(d).wait_recv())

    def xx(d):
        return send(dv.at[slot], dv.at[slot], xs.at[d], xr.at[d], *xpeer(d))

    def cc(d):
        at = c * X + rem(x - d + X, X)
        return send(dv.at[at], dv.at[at], cs.at[d], cr.at[d], seq, sibling)

    loop(1, X, lambda d: xx(d).start())
    cc(0).start()

    def on(d):
        xx(d).wait_recv()
        cc(d).start()

    loop(1, X, on)
    loop(0, X, lambda d: cc(d).wait_recv())

    tokens = PP * TOK
    right = cols[...].reshape(tokens, feat)
    wide = min(512, dv.shape[2])
    heads = wide // HD

    def product(i):
        left = dv[:, :, aligned(i * wide, wide)].reshape(tokens, wide)
        g = contract(left, right, 0, 0).astype(BF16).reshape(heads, Y, rows, feat)
        for a in range(heads):
            for b in range(Y):
                gp[b, i * heads + a] = g[a, b]

    loop(0, dv.shape[2] // wide, product)

    def y2(e):
        return send(gp.at[rem(y + e, Y)], gy.at[e], y2s.at[e], y2r.at[e], *ypeer(e))

    loop(1, Y, lambda e: y2(e).start())
    loop(1, Y, lambda e: y2(e).wait_recv())

    def z2(d):
        to = rem(z + d, Z)
        return send(gz.at[to], gr.at[d], z2s.at[d], z2r.at[d], to * Y + y, dp)

    def sum_at(to):
        block = gp[y, to].astype(F32)
        for e in range(1, Y):
            block = block + gy[e, to].astype(F32)
        return block

    def sum_send(d):
        to = rem(z + d, Z)
        gz[to] = sum_at(to).astype(BF16)
        z2(d).start()

    loop(1, Z, sum_send)
    total = sum_at(z)
    for d in range(1, Z):
        z2(d).wait_recv()
        total = total + gr[d].astype(F32)
    fresh = total * total / (n.S * TOK * PP)
    estimate[...] = fresh
    updated[...] = beta_two * hessian[...] + (1.0 - beta_two) * fresh

    loop(1, Y, lambda e: y1(e).wait_send())
    loop(1, Z, lambda d: z1(d).wait_send())
    loop(1, X, lambda d: xx(d).wait_send())
    loop(0, X, lambda d: cc(d).wait_send())
    loop(1, Y, lambda e: y2(e).wait_send())
    loop(1, Z, lambda d: z2(d).wait_send())


def last(n, grads, cols, hessian):
    dma = pltpu.SemaphoreType.DMA
    rows, feat = hessian.shape
    kv = n.Z * HD
    out = jax.ShapeDtypeStruct(hessian.shape, F32)
    return pl.pallas_call(
        functools.partial(last_kernel, n),
        out_shape=(out, out),
        in_specs=[VMEM] * 3,
        out_specs=(VMEM, VMEM),
        scratch_shapes=[
            pltpu.VMEM((n.Y, n.Z, TOK, HD), BF16),
            pltpu.VMEM((n.Z, TOK, HD), BF16),
            pltpu.VMEM((n.P, TOK, kv), BF16),
            pltpu.VMEM((n.Y, n.Z, rows, feat), BF16),
            pltpu.VMEM((n.Y, n.Z, rows, feat), BF16),
            pltpu.VMEM((n.Z, rows, feat), BF16),
            pltpu.VMEM((n.Z, rows, feat), BF16),
            dma((n.Y,)),
            dma((n.Y,)),
            dma((n.Z,)),
            dma((n.Z,)),
            dma((n.X,)),
            dma((n.X,)),
            dma((n.X,)),
            dma((n.X,)),
            dma((n.Y,)),
            dma((n.Y,)),
            dma((n.Z,)),
            dma((n.Z,)),
            dma((1,)),
        ],
        compiler_params=pltpu.CompilerParams(collective_id=2, has_side_effects=True),
        name="last",
    )(grads, cols, hessian)


def local(queries, keys, hidden, value_weight, readout, base_logits, labels, hessian):
    n = sizes_of(lax.axis_size("seq"), lax.axis_size("dp"))
    cols, qz, kz, vz = front(n, hidden[0], queries[0], keys[0], value_weight)
    z = lax.axis_index("seq") // n.Y
    mine = lax.dynamic_slice_in_dim(readout, z * qz.shape[2], qz.shape[2], 0)
    share, kept, inverse = attend(n, qz, kz.reshape(-1, HD), vz.reshape(-1, HD), mine)
    slopes = logit_slopes(n, share, base_logits[0], labels.reshape(TOK, 1))
    grads = value_grads(n, slopes, mine, kept, inverse)
    return last(n, grads, cols, hessian)


def solution(mesh):
    placed = (
        P("dp", "seq", None),
        P("dp", "seq", None),
        P("dp", "seq", None),
        P("dp", None),
        P(),
        P("dp", "seq", None),
        P("dp", "seq"),
        P("seq", "dp"),
    )
    return jax.shard_map(
        local,
        mesh=mesh,
        in_specs=placed,
        out_specs=(P("seq", "dp"), P("seq", "dp")),
        check_vma=False,
    )
```

```python
import functools
import math
import types

import jax
import jax.numpy as jnp
from jax import lax
from jax.experimental import pallas as pl
from jax.experimental.pallas import tpu as pltpu
from jax.sharding import PartitionSpec as P

HD = 128
TOK = 128
SMALL = -1.0e30
beta_two = 0.99
MESH = pl.DeviceIdType.MESH
F32 = jnp.float32
BF16 = jnp.bfloat16
VMEM = pl.BlockSpec(memory_space=pltpu.VMEM)
ANY = pl.BlockSpec(memory_space=pl.ANY)


def sizes_of(seq, dp):
    n = types.SimpleNamespace(S=seq, P=dp, C=2, X=dp // 2)
    n.Y = 4 if seq == 32 else 2
    n.Z = seq // n.Y
    return n


def place():
    return lax.axis_index("seq"), lax.axis_index("dp")


def rem(a, b):
    return lax.rem(a, jnp.int32(b))


def loop(low, high, step):
    def body(i, carry):
        step(i)
        return carry

    lax.fori_loop(low, high, body, 0)


def aligned(start, size):
    return pl.ds(pl.multiple_of(start, size), size)


def send(src, dst, send_sem, recv_sem, seq, dp):
    return pltpu.make_async_remote_copy(
        src_ref=src,
        dst_ref=dst,
        send_sem=send_sem,
        recv_sem=recv_sem,
        device_id=(seq, dp),
        device_id_type=MESH,
    )


def greet(peers):
    barrier = pltpu.get_barrier_semaphore()
    count = 0
    for low, high, where in peers:

        def one(d, where=where):
            seq, dp = where(d)
            pl.semaphore_signal(barrier, inc=1, device_id=(seq, dp), device_id_type=MESH)

        loop(low, high, one)
        count += high - low
    pl.semaphore_wait(barrier, count)


def contract(a, b, da, db):
    return lax.dot_general(a, b, (((da,), (db,)), ((), ())), preferred_element_type=F32)


def whole_kernel(n, names, hidden, queries, keys, weight_in, readout_in, base, labels, result, *scratch):
    r = types.SimpleNamespace(**dict(zip(names, scratch, strict=True)))
    seq, dp = place()
    Z, Y, X, C, PP = n.Z, n.Y, n.X, n.C, n.P
    z, y = seq // Y, rem(seq, Y)
    x, c = dp // C, rem(dp, C)
    feat = hidden.shape[1] // PP
    qw = queries.shape[1] // Z
    kv = keys.shape[1]
    group = qw // HD
    chunk = Y * TOK
    wide = group * TOK
    sibling = x * C + 1 - c
    slot = c * X + x

    def zpeer(d):
        return rem(z + d, Z) * Y + y, dp

    def ypeer(e):
        return z * Y + rem(y + e, Y), dp

    def ppeer(d):
        return seq, rem(dp + d, PP)

    def xpeer(d):
        return seq, rem(x + d, X) * C + c

    def lanes(ref, i, width):
        return ref.at[:, aligned(i * width, width)]

    get_weight = pltpu.make_async_copy(weight_in, r.weight, r.loc.at[4])
    get_readout = pltpu.make_async_copy(readout_in.at[aligned(z * qw, qw)], r.readout, r.loc.at[5])
    own_k = pltpu.make_async_copy(lanes(keys, z, HD), r.kz.at[seq], r.loc.at[0])
    own_h = pltpu.make_async_copy(lanes(hidden, dp, feat), r.cols.at[slot], r.loc.at[1])
    own_q = pltpu.make_async_copy(lanes(queries, z, qw), r.qz.at[z], r.loc.at[2])
    for own in (own_k, own_h, own_q, get_weight, get_readout):
        own.start()

    greet(((1, Z, zpeer), (1, Y, ypeer), (1, PP, ppeer)))


    def k_send(d):
        to = rem(z + d, Z)
        return send(lanes(keys, to, HD), r.kz.at[seq], r.ks.at[d], r.kr.at[d], to * Y + y, dp)

    def h_send(d):
        to = rem(dp + d, PP)
        return send(lanes(hidden, to, feat), r.cols.at[slot], r.hs.at[d], r.hr.at[d], seq, to)

    def q_send(d):
        to = rem(z + d, Z)
        return send(lanes(queries, to, qw), r.qz.at[z], r.qs.at[d], r.qr.at[d], to * Y + y, dp)

    loop(1, Z, lambda d: k_send(d).start())
    loop(1, PP, lambda d: h_send(d).start())
    loop(1, Z, lambda d: q_send(d).start())

    def forward(ref, first, d, e, ssem, rsem):
        at = rem(z - d + Z, Z) * Y + y
        src = first if first is not None else ref.at[at]
        return send(src, ref.at[at], ssem.at[d, e], rsem.at[d, e], *ypeer(e))

    def k_forward(first, d, e):
        return forward(r.kz, first, d, e, r.kys, r.kyr)

    def v_forward(first, d, e):
        return forward(r.vz, first, d, e, r.vys, r.vyr)

    def v_send(d):
        to = rem(z + d, Z)
        return send(lanes(r.val, to, HD), r.vz.at[seq], r.vs.at[d], r.vr.at[d], to * Y + y, dp)

    def pass_on(sent, via, d):
        sent(d).wait_recv()
        loop(1, Y, lambda e: via(None, d, e).start())

    k_mine = lanes(keys, z, HD)
    v_mine = lanes(r.val, z, HD)
    loop(1, Y, lambda e: k_forward(k_mine, 0, e).start())
    loop(1, Z, lambda d: pass_on(k_send, k_forward, d))


    get_weight.wait()
    own_h.wait()
    loop(1, PP, lambda d: h_send(d).wait_recv())
    rows = X * TOK
    width = min(512, kv)

    def product(half):
        block = r.cols[pl.ds(half * X, X)].reshape(rows, feat)

        def piece(w):
            r.part[aligned(half * rows, rows), aligned(w * width, width)] = jnp.dot(
                block, r.weight[:, aligned(w * width, width)], preferred_element_type=F32
            ).astype(BF16)

        loop(0, kv // width, piece)

    other = 1 - c

    def c_send(i):
        row = aligned((other * X + i) * TOK, TOK)
        return send(r.part.at[row], r.pair.at[i], r.cs.at[i], r.cr.at[i], seq, sibling)

    product(other)
    loop(0, X, lambda i: c_send(i).start())
    product(c)

    def x_send(d):
        to = rem(x + d, X)
        return send(r.both.at[to], r.xin.at[d], r.xs.at[d], r.xr.at[d], seq, to * C + c)

    def join(d):
        to = rem(x + d, X)
        c_send(to).wait_recv()
        mine = r.part[aligned((c * X + to) * TOK, TOK)].astype(F32)
        r.both[to] = (mine + r.pair[to].astype(F32)).astype(BF16)

    def join_send(d):
        join(d)
        x_send(d).start()

    def join_all():
        loop(1, X, join_send)
        join(jnp.int32(X))

    own_v = pltpu.make_async_copy(v_mine, r.vz.at[seq], r.loc.at[3])

    def values_out():
        total = r.both[x].astype(F32)
        for d in range(1, X):
            x_send(d).wait_recv()
            total = total + r.xin[d].astype(F32)
        r.val[...] = total.astype(BF16)
        loop(1, Z, lambda d: v_send(d).start())
        own_v.start()
        loop(1, Y, lambda e: v_forward(v_mine, 0, e).start())


    own_k.wait()
    own_q.wait()
    loop(1, Y, lambda e: k_forward(k_mine, 0, e).wait_recv())
    loop(1, Z, lambda d: loop(1, Y, lambda e: k_forward(None, d, e).wait_recv()))
    factor = math.log2(math.e) / math.sqrt(HD)

    def fold(a, op):
        return op(a.reshape(chunk // 8, 8, wide), axis=0)

    def keys_of(j):
        return r.kz[pl.ds(j * Y, Y)].reshape(chunk, HD)

    def weights_of(t):
        q_block = r.qz[t]
        q_rows = jnp.concatenate([q_block[:, h * HD : (h + 1) * HD] for h in range(group)], axis=0)
        at = t * (t + 1) // 2

        def first(j, peak):
            s = contract(keys_of(j), q_rows, 1, 1)
            r.raw[aligned(j * chunk, chunk), :] = s
            return jnp.maximum(peak, fold(s, jnp.max))

        s = contract(keys_of(t), q_rows, 1, 1)
        key_at = lax.broadcasted_iota(jnp.int32, (chunk, wide), 0)
        query_at = lax.broadcasted_iota(jnp.int32, (chunk, wide), 1)
        s = jnp.where(key_at <= (query_at & (TOK - 1)) + y * TOK, s, SMALL)
        r.raw[aligned(t * chunk, chunk), :] = s
        peak = lax.fori_loop(0, t, first, fold(s, jnp.max))
        peak = jnp.max(peak, axis=0, keepdims=True)

        def second(j, total):
            e = jnp.exp2((r.raw[aligned(j * chunk, chunk), :] - peak) * factor)
            r.kept[at + j] = e.astype(BF16)
            return total + fold(e, jnp.sum)

        total = lax.fori_loop(0, t + 1, second, jnp.zeros((8, wide), F32))
        scale = 1.0 / jnp.sum(total, axis=0, keepdims=True)
        r.inverse[t] = jnp.broadcast_to(scale, (8, wide))

    steps = {}
    steps.setdefault(min(1, Z - 1), []).append(join_all)
    steps.setdefault(min(3, Z - 1), []).append(values_out)

    def score_step(d):
        @pl.when(d > 0)
        def _():
            q_send(d).wait_recv()

        weights_of(rem(z - d + Z, Z))
        for at, calls in steps.items():

            @pl.when(d == at)
            def _(calls=calls):
                for call in calls:
                    call()

    early = max(1, Z - 2)
    loop(0, early, score_step)
    if early <= 3 and Z - 1 >= early:
        loop(early, Z, score_step)
        loop(1, Z, lambda d: pass_on(v_send, v_forward, d))
    else:
        loop(1, Z, lambda d: pass_on(v_send, v_forward, d))
        loop(early, Z, score_step)


    get_readout.wait()
    own_v.wait()
    loop(1, Y, lambda e: v_forward(v_mine, 0, e).wait_recv())
    loop(1, Z, lambda d: loop(1, Y, lambda e: v_forward(None, d, e).wait_recv()))

    def turn(j):
        r.vt[j] = r.vz[pl.ds(j * Y, Y)].reshape(chunk, HD).astype(F32).T.astype(BF16)

    loop(0, Z, turn)

    def l_send(d):
        to = rem(z + d, Z)
        return send(r.share.at[to], r.arrived.at[d], r.ls.at[d], r.lr.at[d], to * Y + y, dp)

    def share_step(i):
        t = rem(z + i, Z)
        at = t * (t + 1) // 2
        r.out[...] = jnp.zeros_like(r.out)

        def add(j):
            r.out[...] += jnp.dot(r.vt[j], r.kept[at + j], preferred_element_type=F32)

        loop(0, t + 1, add)
        mixed = (r.out[...] * r.inverse[t][:1]).astype(BF16)
        part = jnp.zeros((TOK, r.readout.shape[1]), F32)
        for h in range(group):
            at = slice(h * HD, (h + 1) * HD)
            part = part + contract(mixed[:, at], r.readout[at, :], 0, 0)
        r.share[t] = part.astype(BF16)

        @pl.when(i < Z)
        def _():
            l_send(i).start()

    loop(1, Z + 1, share_step)

    total = base[...] + r.share[z].astype(F32)
    for d in range(1, Z):
        l_send(d).wait_recv()
        total = total + r.arrived[d].astype(F32)
    peak = jnp.max(total, axis=1, keepdims=True)
    e = jnp.exp(total - peak)
    soft = e / jnp.sum(e, axis=1, keepdims=True)
    label = jnp.broadcast_to(labels[...].astype(F32), (8, TOK)).T[:, :1]
    column = lax.broadcasted_iota(jnp.int32, total.shape, 1).astype(F32)
    r.slopes[z] = (soft - jnp.where(label == column, 1.0, 0.0)).astype(BF16)

    def s_send(d):
        return send(r.slopes.at[z], r.slopes.at[z], r.ss.at[d], r.sr.at[d], *zpeer(d))

    loop(1, Z, lambda d: s_send(d).start())

    def slope_step(d):
        @pl.when(d > 0)
        def _():
            s_send(d).wait_recv()

        t = rem(z - d + Z, Z)
        slope = r.slopes[t]
        for h in range(group):
            at = slice(h * HD, (h + 1) * HD)
            column = r.inverse[t][:, at].T[:, :1]
            r.d_rows[t, at, :] = (contract(slope, r.readout[at, :], 1, 1) * column).astype(BF16)

    loop(0, Z, slope_step)


    tokens = PP * TOK
    quarter = HD // Y

    def head_lanes(ref, h):
        return ref.at[:, aligned(h * HD, HD)]

    def y1(i, e):
        to = rem(y + e, Y)
        return send(r.grads.at[i, to], r.ya.at[i, e], r.y1s.at[i, e], r.y1r.at[i, e], *ypeer(e))

    def stage0(i):
        j = rem(z + i, Z)
        r.acc[...] = jnp.zeros_like(r.acc)

        def add(t):
            r.acc[...] += jnp.dot(
                r.kept[t * (t + 1) // 2 + j], r.d_rows[t], preferred_element_type=F32
            )

        loop(j, Z, add)
        for b in range(Y):
            r.grads[i, b] = r.acc[b * TOK : (b + 1) * TOK, :].astype(BF16)
        loop(1, Y, lambda e: y1(i, e).start())

    def z1(i):
        to = rem(z + i, Z)
        dst = head_lanes(r.dv.at[slot], z)
        return send(r.dz.at[i], dst, r.z1s.at[i], r.z1r.at[i], to * Y + y, dp)

    own_dv = pltpu.make_async_copy(r.dz.at[Z], head_lanes(r.dv.at[slot], z), r.loc.at[6])

    def stage1(i):
        loop(1, Y, lambda e: y1(i, e).wait_recv())
        block = r.grads[i, y].astype(F32)
        for e in range(1, Y):
            block = block + r.ya[i, e].astype(F32)
        r.dz[i] = block.astype(BF16)

        @pl.when(i < Z)
        def _():
            z1(i).start()

        @pl.when(i == Z)
        def _():
            own_dv.start()

    def head_at(i):
        return rem(z - i + Z, Z)

    def xx(i, d):
        ref = head_lanes(r.dv.at[slot], head_at(i))
        return send(ref, ref, r.x2s.at[i, d], r.x2r.at[i, d], *xpeer(d))

    def cc(i, d):
        at = c * X + rem(x - d + X, X)
        ref = head_lanes(r.dv.at[at], head_at(i))
        return send(ref, ref, r.c2s.at[i, d], r.c2r.at[i, d], seq, sibling)

    def stage2(i):
        @pl.when(i < Z)
        def _():
            z1(i).wait_recv()

        @pl.when(i == Z)
        def _():
            own_dv.wait()

        loop(1, X, lambda d: xx(i, d).start())
        cc(i, 0).start()

    def stage3(i):
        def on(d):
            xx(i, d).wait_recv()
            cc(i, d).start()

        loop(1, X, on)

    def y2(i, e):
        to = rem(y + e, Y)
        return send(r.gp.at[i, to], r.gy.at[i, e], r.y2s.at[i, e], r.y2r.at[i, e], *ypeer(e))

    def stage4(i):
        loop(0, X, lambda d: cc(i, d).wait_recv())
        left = r.dv[:, :, aligned(head_at(i) * HD, HD)].reshape(tokens, HD)
        right = r.cols[...].reshape(tokens, feat)
        r.gp[i] = contract(left, right, 0, 0).astype(BF16).reshape(Y, quarter, feat)
        loop(1, Y, lambda e: y2(i, e).start())

    def z2(i):
        return send(r.gz.at[i], r.gr.at[i], r.z2s.at[i], r.z2r.at[i], head_at(i) * Y + y, dp)

    def stage5(i):
        loop(1, Y, lambda e: y2(i, e).wait_recv())
        block = r.gp[i, y].astype(F32)
        for e in range(1, Y):
            block = block + r.gy[i, e].astype(F32)

        @pl.when(i < Z)
        def _():
            r.gz[i] = block.astype(BF16)
            z2(i).start()

        @pl.when(i == Z)
        def _():
            r.own[...] = block

    r.sum[...] = jnp.zeros_like(r.sum)

    def stage6(i):
        @pl.when(i < Z)
        def _():
            z2(i).wait_recv()
            r.sum[...] += r.gr[i].astype(F32)

    stages = (stage0, stage1, stage2, stage3, stage4, stage5, stage6)

    def tick(k):
        for s, stage in enumerate(stages):

            @pl.when((k - s >= 1) & (k - s <= Z))
            def _(s=s, stage=stage):
                stage(k - s)

    loop(1, Z + len(stages), tick)
    result[...] = r.sum[...] + r.own[...]


    def drain(i):
        loop(1, Y, lambda e: k_forward(None, i, e).wait_send())
        loop(1, Y, lambda e: v_forward(None, i, e).wait_send())
        for sent in (k_send, q_send, v_send, l_send, s_send, z1, z2):
            sent(i).wait_send()

    loop(1, Z, drain)
    loop(1, Y, lambda e: k_forward(k_mine, 0, e).wait_send())
    loop(1, Y, lambda e: v_forward(v_mine, 0, e).wait_send())
    loop(1, PP, lambda d: h_send(d).wait_send())
    loop(0, X, lambda i: c_send(i).wait_send())
    loop(1, X, lambda d: x_send(d).wait_send())

    def drain_late(i):
        loop(1, Y, lambda e: y1(i, e).wait_send())
        loop(1, Y, lambda e: y2(i, e).wait_send())
        loop(1, X, lambda d: xx(i, d).wait_send())
        loop(0, X, lambda d: cc(i, d).wait_send())

    loop(1, Z + 1, drain_late)


def whole(n, hidden, queries, keys, weight, readout, base, labels, rows):
    Z, Y, X, PP = n.Z, n.Y, n.X, n.P
    feat = hidden.shape[1] // PP
    qw = queries.shape[1] // Z
    kv = keys.shape[1]
    cand = readout.shape[1]
    chunk = Y * TOK
    dma = pltpu.SemaphoreType.DMA
    vmem = pltpu.VMEM
    scratch = dict(
        weight=vmem((feat, kv), BF16),
        readout=vmem((qw, cand), BF16),
        cols=vmem((PP, TOK, feat), BF16),
        qz=vmem((Z, TOK, qw), BF16),
        kz=vmem((n.S, TOK, HD), BF16),
        vz=vmem((n.S, TOK, HD), BF16),
        part=vmem((PP * TOK, kv), BF16),
        pair=vmem((X, TOK, kv), BF16),
        both=vmem((X, TOK, kv), BF16),
        xin=vmem((X, TOK, kv), BF16),
        val=vmem((TOK, kv), BF16),
        raw=vmem((Z * chunk, qw), F32),
        vt=vmem((Z, HD, chunk), BF16),
        out=vmem((HD, qw), F32),
        kept=vmem((Z * (Z + 1) // 2, chunk, qw), BF16),
        inverse=vmem((Z, 8, qw), F32),
        share=vmem((Z, TOK, cand), BF16),
        arrived=vmem((Z, TOK, cand), BF16),
        slopes=vmem((Z, TOK, cand), BF16),
        d_rows=vmem((Z, qw, HD), BF16),
        acc=vmem((chunk, HD), F32),
        grads=vmem((Z + 1, Y, TOK, HD), BF16),
        ya=vmem((Z + 1, Y, TOK, HD), BF16),
        dz=vmem((Z + 1, TOK, HD), BF16),
        dv=vmem((PP, TOK, kv), BF16),
        gp=vmem((Z + 1, Y, rows, feat), BF16),
        gy=vmem((Z + 1, Y, rows, feat), BF16),
        gz=vmem((Z, rows, feat), BF16),
        gr=vmem((Z, rows, feat), BF16),
        sum=vmem((rows, feat), F32),
        own=vmem((rows, feat), F32),
        loc=dma((7,)),
    )
    for name in ("h",):
        scratch |= {name + "s": dma((PP,)), name + "r": dma((PP,))}
    for name in ("k", "q", "v", "l", "s", "z1", "z2"):
        scratch |= {name + "s": dma((Z,)), name + "r": dma((Z,))}
    for name in ("c", "x"):
        scratch |= {name + "s": dma((X,)), name + "r": dma((X,))}
    for name in ("ky", "vy"):
        scratch |= {name + "s": dma((Z, Y)), name + "r": dma((Z, Y))}
    for name in ("y1", "y2"):
        scratch |= {name + "s": dma((Z + 1, Y)), name + "r": dma((Z + 1, Y))}
    for name in ("x2", "c2"):
        scratch |= {name + "s": dma((Z + 1, X)), name + "r": dma((Z + 1, X))}
    return pl.pallas_call(
        functools.partial(whole_kernel, n, tuple(scratch)),
        out_shape=jax.ShapeDtypeStruct((rows, feat), F32),
        in_specs=[ANY, ANY, ANY, ANY, ANY, VMEM, VMEM],
        out_specs=VMEM,
        scratch_shapes=list(scratch.values()),
        compiler_params=pltpu.CompilerParams(
            collective_id=0, has_side_effects=True, vmem_limit_bytes=64 * 1024 * 1000
        ),
        name="whole",
    )(hidden, queries, keys, weight, readout, base, labels)


def local(queries, keys, hidden, value_weight, readout, base_logits, labels, hessian):
    n = sizes_of(lax.axis_size("seq"), lax.axis_size("dp"))
    total = whole(
        n,
        hidden[0],
        queries[0],
        keys[0],
        value_weight,
        readout,
        base_logits[0],
        labels,
        hessian.shape[0],
    )
    estimate = total * total / (n.S * TOK * n.P)
    return estimate, beta_two * hessian + (1.0 - beta_two) * estimate


def solution(mesh):
    placed = (
        P("dp", "seq", None),
        P("dp", "seq", None),
        P("dp", "seq", None),
        P("dp", None),
        P(),
        P("dp", "seq", None),
        P("dp", "seq"),
        P("seq", "dp"),
    )
    return jax.shard_map(
        local,
        mesh=mesh,
        in_specs=placed,
        out_specs=(P("seq", "dp"), P("seq", "dp")),
        check_vma=False,
    )
```

```python
import functools
import math
import types

import jax
import jax.numpy as jnp
from jax import lax
from jax.experimental import pallas as pl
from jax.experimental.pallas import tpu as pltpu
from jax.sharding import PartitionSpec as P

HD = 128
TOK = 128
SMALL = -1.0e30
beta_two = 0.99
MESH = pl.DeviceIdType.MESH
F32 = jnp.float32
BF16 = jnp.bfloat16
VMEM = pl.BlockSpec(memory_space=pltpu.VMEM)
ANY = pl.BlockSpec(memory_space=pl.ANY)


def sizes_of(seq, dp):
    n = types.SimpleNamespace(S=seq, P=dp, C=2, X=dp // 2)
    n.Y = 4 if seq == 32 else 2
    n.Z = seq // n.Y
    return n


def place():
    return lax.axis_index("seq"), lax.axis_index("dp")


def rem(a, b):
    return lax.rem(a, jnp.int32(b))


def loop(low, high, step):
    def body(i, carry):
        step(i)
        return carry

    lax.fori_loop(low, high, body, 0)


def aligned(start, size):
    return pl.ds(pl.multiple_of(start, size), size)


def send(src, dst, send_sem, recv_sem, seq, dp):
    return pltpu.make_async_remote_copy(
        src_ref=src,
        dst_ref=dst,
        send_sem=send_sem,
        recv_sem=recv_sem,
        device_id=(seq, dp),
        device_id_type=MESH,
    )


def greet(peers):
    barrier = pltpu.get_barrier_semaphore()
    count = 0
    for low, high, where in peers:

        def one(d, where=where):
            seq, dp = where(d)
            pl.semaphore_signal(barrier, inc=1, device_id=(seq, dp), device_id_type=MESH)

        loop(low, high, one)
        count += high - low
    pl.semaphore_wait(barrier, count)


def contract(a, b, da, db):
    return lax.dot_general(a, b, (((da,), (db,)), ((), ())), preferred_element_type=F32)


def whole_kernel(n, names, hidden, queries, keys, weight_in, readout_in, base, labels, result, *scratch):
    r = types.SimpleNamespace(**dict(zip(names, scratch, strict=True)))
    seq, dp = place()
    Z, Y, X, C, PP = n.Z, n.Y, n.X, n.C, n.P
    z, y = seq // Y, rem(seq, Y)
    x, c = dp // C, rem(dp, C)
    feat = hidden.shape[1] // PP
    qw = queries.shape[1] // Z
    kv = keys.shape[1]
    group = qw // HD
    chunk = Y * TOK
    wide = group * TOK
    sibling = x * C + 1 - c
    slot = c * X + x

    def zpeer(d):
        return rem(z + d, Z) * Y + y, dp

    def ypeer(e):
        return z * Y + rem(y + e, Y), dp

    def ppeer(d):
        return seq, rem(dp + d, PP)

    def xpeer(d):
        return seq, rem(x + d, X) * C + c

    def lanes(ref, i, width):
        return ref.at[:, aligned(i * width, width)]

    get_weight = pltpu.make_async_copy(weight_in, r.weight, r.loc.at[4])
    get_readout = pltpu.make_async_copy(readout_in.at[aligned(z * qw, qw)], r.readout, r.loc.at[5])
    own_k = pltpu.make_async_copy(lanes(keys, z, HD), r.kz.at[seq], r.loc.at[0])
    own_h = pltpu.make_async_copy(lanes(hidden, dp, feat), r.cols.at[slot], r.loc.at[1])
    own_q = pltpu.make_async_copy(lanes(queries, z, qw), r.qz.at[z], r.loc.at[2])
    for own in (own_k, own_h, own_q, get_weight, get_readout):
        own.start()

    greet(((1, Z, zpeer), (1, Y, ypeer), (1, PP, ppeer)))


    def k_send(d):
        to = rem(z + d, Z)
        return send(lanes(keys, to, HD), r.kz.at[seq], r.ks.at[d], r.kr.at[d], to * Y + y, dp)

    def h_send(d):
        to = rem(dp + d, PP)
        return send(lanes(hidden, to, feat), r.cols.at[slot], r.hs.at[d], r.hr.at[d], seq, to)

    def q_send(d):
        to = rem(z + d, Z)
        return send(lanes(queries, to, qw), r.qz.at[z], r.qs.at[d], r.qr.at[d], to * Y + y, dp)

    loop(1, Z, lambda d: k_send(d).start())
    loop(1, PP, lambda d: h_send(d).start())
    loop(1, Z, lambda d: q_send(d).start())

    def forward(ref, first, d, e, ssem, rsem):
        at = rem(z - d + Z, Z) * Y + y
        src = first if first is not None else ref.at[at]
        return send(src, ref.at[at], ssem.at[d, e], rsem.at[d, e], *ypeer(e))

    def k_forward(first, d, e):
        return forward(r.kz, first, d, e, r.kys, r.kyr)

    def v_forward(first, d, e):
        return forward(r.vz, first, d, e, r.vys, r.vyr)

    def v_send(d):
        return send(r.val.at[d], r.vz.at[seq], r.vs.at[d], r.vr.at[d], *zpeer(d))

    def pass_on(sent, via, d):
        sent(d).wait_recv()
        loop(1, Y, lambda e: via(None, d, e).start())

    k_mine = lanes(keys, z, HD)
    v_mine = r.val.at[Z]
    loop(1, Y, lambda e: k_forward(k_mine, 0, e).start())
    loop(1, Z, lambda d: pass_on(k_send, k_forward, d))


    get_weight.wait()
    own_h.wait()
    loop(1, PP, lambda d: h_send(d).wait_recv())
    half = X * TOK
    other = 1 - c

    def c_send(i):
        src = r.part.at[i, aligned(other * half, half)]
        return send(src, r.pair.at[i], r.cs.at[i], r.cr.at[i], seq, sibling)

    def product(i):
        head = rem(z + i, Z)
        block = r.cols[...].reshape(PP * TOK, feat)
        r.part[i] = jnp.dot(
            block, r.weight[:, aligned(head * HD, HD)], preferred_element_type=F32
        ).astype(BF16)
        c_send(i).start()

    loop(1, Z + 1, product)

    def x_send(i, d):
        to = rem(x + d, X)
        src = r.both.at[i, aligned(to * TOK, TOK)]
        return send(src, r.xin.at[i, d], r.xs.at[i, d], r.xr.at[i, d], seq, to * C + c)

    def join(i):
        c_send(i).wait_recv()
        mine = r.part[i, aligned(c * half, half)].astype(F32)
        r.both[i] = (mine + r.pair[i].astype(F32)).astype(BF16)
        loop(1, X, lambda d: x_send(i, d).start())

    def values_out(i):
        total = r.both[i, aligned(x * TOK, TOK)].astype(F32)
        for d in range(1, X):
            x_send(i, d).wait_recv()
            total = total + r.xin[i, d].astype(F32)
        block = total.astype(BF16)
        r.val[i] = block

        @pl.when(i < Z)
        def _():
            v_send(i).start()

        @pl.when(i == Z)
        def _():
            r.vz[seq] = block

    def values_on(i):
        @pl.when(i < Z)
        def _():
            pass_on(v_send, v_forward, i)

        @pl.when(i == Z)
        def _():
            loop(1, Y, lambda e: v_forward(v_mine, i, e).start())


    own_k.wait()
    own_q.wait()
    loop(1, Y, lambda e: k_forward(k_mine, 0, e).wait_recv())
    loop(1, Z, lambda d: loop(1, Y, lambda e: k_forward(None, d, e).wait_recv()))
    factor = math.log2(math.e) / math.sqrt(HD)

    def fold(a, op):
        return op(a.reshape(chunk // 8, 8, wide), axis=0)

    def keys_of(j):
        return r.kz[pl.ds(j * Y, Y)].reshape(chunk, HD)

    def weights_of(t):
        q_block = r.qz[t]
        q_rows = jnp.concatenate([q_block[:, h * HD : (h + 1) * HD] for h in range(group)], axis=0)
        at = t * (t + 1) // 2

        def first(j, peak):
            s = contract(keys_of(j), q_rows, 1, 1)
            r.raw[aligned(j * chunk, chunk), :] = s
            return jnp.maximum(peak, fold(s, jnp.max))

        s = contract(keys_of(t), q_rows, 1, 1)
        key_at = lax.broadcasted_iota(jnp.int32, (chunk, wide), 0)
        query_at = lax.broadcasted_iota(jnp.int32, (chunk, wide), 1)
        s = jnp.where(key_at <= (query_at & (TOK - 1)) + y * TOK, s, SMALL)
        r.raw[aligned(t * chunk, chunk), :] = s
        peak = lax.fori_loop(0, t, first, fold(s, jnp.max))
        peak = jnp.max(peak, axis=0, keepdims=True)

        def second(j, total):
            e = jnp.exp2((r.raw[aligned(j * chunk, chunk), :] - peak) * factor)
            r.kept[at + j] = e.astype(BF16)
            return total + fold(e, jnp.sum)

        total = lax.fori_loop(0, t + 1, second, jnp.zeros((8, wide), F32))
        scale = 1.0 / jnp.sum(total, axis=0, keepdims=True)
        r.inverse[t] = jnp.broadcast_to(scale, (8, wide))

    values_stages = (join, values_out, values_on)

    def front_tick(m):
        for at, stage in enumerate(values_stages):

            @pl.when((m >= at) & (m - at < Z // 2))
            def _(at=at, stage=stage):
                stage(2 * (m - at) + 1)
                stage(2 * (m - at) + 2)

        @pl.when((m > 0) & (m < Z))
        def _():
            q_send(m).wait_recv()

        @pl.when(m < Z)
        def _():
            weights_of(rem(z - m + Z, Z))

    loop(0, max(Z, Z // 2 + len(values_stages) - 1), front_tick)


    def drain_front():
        loop(1, Y, lambda e: k_forward(k_mine, 0, e).wait_send())
        loop(1, Y, lambda e: v_forward(v_mine, Z, e).wait_send())
        loop(1, PP, lambda d: h_send(d).wait_send())

        def both_ways(i):
            c_send(i).wait_send()
            loop(1, X, lambda d: x_send(i, d).wait_send())

        loop(1, Z + 1, both_ways)

        def one(i):
            loop(1, Y, lambda e: k_forward(None, i, e).wait_send())
            loop(1, Y, lambda e: v_forward(None, i, e).wait_send())
            for sent in (k_send, q_send, v_send):
                sent(i).wait_send()

        loop(1, Z, one)


    get_readout.wait()
    loop(1, Y, lambda e: v_forward(v_mine, Z, e).wait_recv())
    loop(1, Z, lambda d: loop(1, Y, lambda e: v_forward(None, d, e).wait_recv()))

    def turn(j):
        r.vt[j] = r.vz[pl.ds(j * Y, Y)].reshape(chunk, HD).astype(F32).T.astype(BF16)

    loop(0, Z, turn)

    def l_send(d):
        to = rem(z + d, Z)
        return send(r.share.at[to], r.arrived.at[d], r.ls.at[d], r.lr.at[d], to * Y + y, dp)

    def share_step(i):
        t = rem(z + i, Z)
        at = t * (t + 1) // 2
        r.out[...] = jnp.zeros_like(r.out)

        def add(j):
            r.out[...] += jnp.dot(r.vt[j], r.kept[at + j], preferred_element_type=F32)

        loop(0, t + 1, add)
        mixed = (r.out[...] * r.inverse[t][:1]).astype(BF16)
        part = jnp.zeros((TOK, r.readout.shape[1]), F32)
        for h in range(group):
            at = slice(h * HD, (h + 1) * HD)
            part = part + contract(mixed[:, at], r.readout[at, :], 0, 0)
        r.share[t] = part.astype(BF16)

        @pl.when(i < Z)
        def _():
            l_send(i).start()

    loop(1, Z + 1, share_step)

    total = base[...] + r.share[z].astype(F32)
    for d in range(1, Z):
        l_send(d).wait_recv()
        total = total + r.arrived[d].astype(F32)
    peak = jnp.max(total, axis=1, keepdims=True)
    e = jnp.exp(total - peak)
    soft = e / jnp.sum(e, axis=1, keepdims=True)
    label = jnp.broadcast_to(labels[...].astype(F32), (8, TOK)).T[:, :1]
    column = lax.broadcasted_iota(jnp.int32, total.shape, 1).astype(F32)
    r.slopes[z] = (soft - jnp.where(label == column, 1.0, 0.0)).astype(BF16)

    def s_send(d):
        return send(r.slopes.at[z], r.slopes.at[z], r.ss.at[d], r.sr.at[d], *zpeer(d))

    loop(1, Z, lambda d: s_send(d).start())

    def slope_step(d):
        @pl.when(d > 0)
        def _():
            s_send(d).wait_recv()

        t = rem(z - d + Z, Z)
        slope = r.slopes[t]
        for h in range(group):
            at = slice(h * HD, (h + 1) * HD)
            column = r.inverse[t][:, at].T[:, :1]
            r.d_rows[t, at, :] = (contract(slope, r.readout[at, :], 1, 1) * column).astype(BF16)

    loop(0, Z, slope_step)

    def drain_middle():
        def one(i):
            l_send(i).wait_send()
            s_send(i).wait_send()

        loop(1, Z, one)


    tokens = PP * TOK
    quarter = HD // Y

    def head_lanes(ref, h):
        return ref.at[:, aligned(h * HD, HD)]

    def y1(i, e):
        to = rem(y + e, Y)
        return send(r.grads.at[i, to], r.ya.at[i, e], r.y1s.at[i, e], r.y1r.at[i, e], *ypeer(e))

    def stage0(i):
        j = rem(z + i, Z)
        r.acc[...] = jnp.zeros_like(r.acc)

        def add(t):
            r.acc[...] += jnp.dot(
                r.kept[t * (t + 1) // 2 + j], r.d_rows[t], preferred_element_type=F32
            )

        loop(j, Z, add)
        for b in range(Y):
            r.grads[i, b] = r.acc[b * TOK : (b + 1) * TOK, :].astype(BF16)
        loop(1, Y, lambda e: y1(i, e).start())

    def z1(i):
        to = rem(z + i, Z)
        dst = head_lanes(r.dv.at[slot], z)
        return send(r.dz.at[i], dst, r.z1s.at[i], r.z1r.at[i], to * Y + y, dp)

    own_dv = pltpu.make_async_copy(r.dz.at[Z], head_lanes(r.dv.at[slot], z), r.loc.at[6])

    def stage1(i):
        loop(1, Y, lambda e: y1(i, e).wait_recv())
        block = r.grads[i, y].astype(F32)
        for e in range(1, Y):
            block = block + r.ya[i, e].astype(F32)
        r.dz[i] = block.astype(BF16)

        @pl.when(i < Z)
        def _():
            z1(i).start()

        @pl.when(i == Z)
        def _():
            own_dv.start()

    def head_at(i):
        return rem(z - i + Z, Z)

    def xx(i, d):
        ref = head_lanes(r.dv.at[slot], head_at(i))
        return send(ref, ref, r.x2s.at[i, d], r.x2r.at[i, d], *xpeer(d))

    def cc(i, d):
        at = c * X + rem(x - d + X, X)
        ref = head_lanes(r.dv.at[at], head_at(i))
        return send(ref, ref, r.c2s.at[i, d], r.c2r.at[i, d], seq, sibling)

    def stage2(i):
        @pl.when(i < Z)
        def _():
            z1(i).wait_recv()

        @pl.when(i == Z)
        def _():
            own_dv.wait()

        loop(1, X, lambda d: xx(i, d).start())
        cc(i, 0).start()

    def stage3(i):
        def on(d):
            xx(i, d).wait_recv()
            cc(i, d).start()

        loop(1, X, on)

    def y2(i, e):
        to = rem(y + e, Y)
        return send(r.gp.at[i, to], r.gy.at[i, e], r.y2s.at[i, e], r.y2r.at[i, e], *ypeer(e))

    def stage4(i):
        loop(0, X, lambda d: cc(i, d).wait_recv())
        left = r.dv[:, :, aligned(head_at(i) * HD, HD)].reshape(tokens, HD)
        right = r.cols[...].reshape(tokens, feat)
        r.gp[i] = contract(left, right, 0, 0).astype(BF16).reshape(Y, quarter, feat)
        loop(1, Y, lambda e: y2(i, e).start())

    def z2(i):
        return send(r.gz.at[i], r.gr.at[i], r.z2s.at[i], r.z2r.at[i], head_at(i) * Y + y, dp)

    def stage5(i):
        loop(1, Y, lambda e: y2(i, e).wait_recv())
        block = r.gp[i, y].astype(F32)
        for e in range(1, Y):
            block = block + r.gy[i, e].astype(F32)

        @pl.when(i < Z)
        def _():
            r.gz[i] = block.astype(BF16)
            z2(i).start()

        @pl.when(i == Z)
        def _():
            r.own[...] = block

    r.sum[...] = jnp.zeros_like(r.sum)

    def stage6(i):
        @pl.when(i < Z)
        def _():
            z2(i).wait_recv()
            r.sum[...] += r.gr[i].astype(F32)

    def drain_last():
        def one(i):
            z1(i).wait_send()
            z2(i).wait_send()

        loop(1, Z, one)

        def more(i):
            loop(1, Y, lambda e: y1(i, e).wait_send())
            loop(1, Y, lambda e: y2(i, e).wait_send())
            loop(1, X, lambda d: xx(i, d).wait_send())
            loop(0, X, lambda d: cc(i, d).wait_send())

        loop(1, Z + 1, more)

    stages = (
        (11, stage6),
        (9, stage5),
        (7, stage4),
        (6, stage3),
        (4, stage2),
        (2, stage1),
        (0, stage0),
    )

    def tick(k):
        for late, stage in stages:

            @pl.when((k - late >= 1) & (k - late <= Z))
            def _(late=late, stage=stage):
                stage(k - late)

    loop(1, Z + 1 + stages[0][0], tick)
    result[...] = r.sum[...] + r.own[...]

    drain_front()
    drain_middle()
    drain_last()


def whole(n, hidden, queries, keys, weight, readout, base, labels, rows):
    Z, Y, X, PP = n.Z, n.Y, n.X, n.P
    feat = hidden.shape[1] // PP
    qw = queries.shape[1] // Z
    kv = keys.shape[1]
    cand = readout.shape[1]
    chunk = Y * TOK
    dma = pltpu.SemaphoreType.DMA
    vmem = pltpu.VMEM
    scratch = dict(
        weight=vmem((feat, kv), BF16),
        readout=vmem((qw, cand), BF16),
        cols=vmem((PP, TOK, feat), BF16),
        qz=vmem((Z, TOK, qw), BF16),
        kz=vmem((n.S, TOK, HD), BF16),
        vz=vmem((n.S, TOK, HD), BF16),
        part=vmem((Z + 1, PP * TOK, HD), BF16),
        pair=vmem((Z + 1, X * TOK, HD), BF16),
        both=vmem((Z + 1, X * TOK, HD), BF16),
        xin=vmem((Z + 1, X, TOK, HD), BF16),
        val=vmem((Z + 1, TOK, HD), BF16),
        raw=vmem((Z * chunk, qw), F32),
        vt=vmem((Z, HD, chunk), BF16),
        out=vmem((HD, qw), F32),
        kept=vmem((Z * (Z + 1) // 2, chunk, qw), BF16),
        inverse=vmem((Z, 8, qw), F32),
        share=vmem((Z, TOK, cand), BF16),
        arrived=vmem((Z, TOK, cand), BF16),
        slopes=vmem((Z, TOK, cand), BF16),
        d_rows=vmem((Z, qw, HD), BF16),
        acc=vmem((chunk, HD), F32),
        grads=vmem((Z + 1, Y, TOK, HD), BF16),
        ya=vmem((Z + 1, Y, TOK, HD), BF16),
        dz=vmem((Z + 1, TOK, HD), BF16),
        dv=vmem((PP, TOK, kv), BF16),
        gp=vmem((Z + 1, Y, rows, feat), BF16),
        gy=vmem((Z + 1, Y, rows, feat), BF16),
        gz=vmem((Z, rows, feat), BF16),
        gr=vmem((Z, rows, feat), BF16),
        sum=vmem((rows, feat), F32),
        own=vmem((rows, feat), F32),
        loc=dma((7,)),
    )
    for name in ("h",):
        scratch |= {name + "s": dma((PP,)), name + "r": dma((PP,))}
    for name in ("k", "q", "v", "l", "s", "z1", "z2"):
        scratch |= {name + "s": dma((Z,)), name + "r": dma((Z,))}
    scratch |= {"cs": dma((Z + 1,)), "cr": dma((Z + 1,))}
    for name in ("ky", "vy", "y1", "y2"):
        scratch |= {name + "s": dma((Z + 1, Y)), name + "r": dma((Z + 1, Y))}
    for name in ("x", "x2", "c2"):
        scratch |= {name + "s": dma((Z + 1, X)), name + "r": dma((Z + 1, X))}
    return pl.pallas_call(
        functools.partial(whole_kernel, n, tuple(scratch)),
        out_shape=jax.ShapeDtypeStruct((rows, feat), F32),
        in_specs=[ANY, ANY, ANY, ANY, ANY, VMEM, VMEM],
        out_specs=VMEM,
        scratch_shapes=list(scratch.values()),
        compiler_params=pltpu.CompilerParams(
            collective_id=0, has_side_effects=True, vmem_limit_bytes=64 * 1024 * 1000
        ),
        name="whole",
    )(hidden, queries, keys, weight, readout, base, labels)


def local(queries, keys, hidden, value_weight, readout, base_logits, labels, hessian):
    n = sizes_of(lax.axis_size("seq"), lax.axis_size("dp"))
    total = whole(
        n,
        hidden[0],
        queries[0],
        keys[0],
        value_weight,
        readout,
        base_logits[0],
        labels,
        hessian.shape[0],
    )
    estimate = total * total / (n.S * TOK * n.P)
    return estimate, beta_two * hessian + (1.0 - beta_two) * estimate


def solution(mesh):
    placed = (
        P("dp", "seq", None),
        P("dp", "seq", None),
        P("dp", "seq", None),
        P("dp", None),
        P(),
        P("dp", "seq", None),
        P("dp", "seq"),
        P("seq", "dp"),
    )
    return jax.shard_map(
        local,
        mesh=mesh,
        in_specs=placed,
        out_specs=(P("seq", "dp"), P("seq", "dp")),
        check_vma=False,
    )
```

```python
import functools
import math
import types

import jax
import jax.numpy as jnp
from jax import lax
from jax.experimental import pallas as pl
from jax.experimental.pallas import tpu as pltpu
from jax.sharding import PartitionSpec as P

HD = 128
TOK = 128
SMALL = -1.0e30
beta_two = 0.99
MESH = pl.DeviceIdType.MESH
F32 = jnp.float32
BF16 = jnp.bfloat16
VMEM = pl.BlockSpec(memory_space=pltpu.VMEM)
ANY = pl.BlockSpec(memory_space=pl.ANY)


def sizes_of(seq, dp):
    n = types.SimpleNamespace(S=seq, P=dp, C=2, X=dp // 2)
    n.Y = 4 if seq == 32 else 2
    n.Z = seq // n.Y
    return n


def place():
    return lax.axis_index("seq"), lax.axis_index("dp")


def rem(a, b):
    return lax.rem(a, jnp.int32(b))


def loop(low, high, step):
    def body(i, carry):
        step(i)
        return carry

    lax.fori_loop(low, high, body, 0)


def aligned(start, size):
    return pl.ds(pl.multiple_of(start, size), size)


def send(src, dst, send_sem, recv_sem, seq, dp):
    return pltpu.make_async_remote_copy(
        src_ref=src,
        dst_ref=dst,
        send_sem=send_sem,
        recv_sem=recv_sem,
        device_id=(seq, dp),
        device_id_type=MESH,
    )


def greet(peers):
    barrier = pltpu.get_barrier_semaphore()
    count = 0
    for low, high, where in peers:

        def one(d, where=where):
            seq, dp = where(d)
            pl.semaphore_signal(barrier, inc=1, device_id=(seq, dp), device_id_type=MESH)

        loop(low, high, one)
        count += high - low
    pl.semaphore_wait(barrier, count)


def contract(a, b, da, db):
    return lax.dot_general(a, b, (((da,), (db,)), ((), ())), preferred_element_type=F32)


def whole_kernel(n, names, hidden, queries, keys, weight_in, readout_in, base, labels, result, *scratch):
    r = types.SimpleNamespace(**dict(zip(names, scratch, strict=True)))
    seq, dp = place()
    Z, Y, X, C, PP = n.Z, n.Y, n.X, n.C, n.P
    z, y = seq // Y, rem(seq, Y)
    x, c = dp // C, rem(dp, C)
    feat = hidden.shape[1] // PP
    qw = queries.shape[1] // Z
    kv = keys.shape[1]
    group = qw // HD
    chunk = Y * TOK
    wide = group * TOK
    sibling = x * C + 1 - c
    slot = c * X + x

    def zpeer(d):
        return rem(z + d, Z) * Y + y, dp

    def ypeer(e):
        return z * Y + rem(y + e, Y), dp

    def ppeer(d):
        return seq, rem(dp + d, PP)

    def xpeer(d):
        return seq, rem(x + d, X) * C + c

    def near(m):
        odd = rem(m, 2)
        return odd * ((m + 1) // 2) + (1 - odd) * rem(Z - m // 2, Z)

    def lanes(ref, i, width):
        return ref.at[:, aligned(i * width, width)]

    get_weight = pltpu.make_async_copy(weight_in, r.weight, r.loc.at[4])
    get_readout = pltpu.make_async_copy(readout_in.at[aligned(z * qw, qw)], r.readout, r.loc.at[5])
    own_k = pltpu.make_async_copy(lanes(keys, z, HD), r.kz.at[seq], r.loc.at[0])
    own_h = pltpu.make_async_copy(lanes(hidden, dp, feat), r.cols.at[slot], r.loc.at[1])
    own_q = pltpu.make_async_copy(lanes(queries, z, qw), r.qz.at[z], r.loc.at[2])
    for own in (own_k, own_h, own_q, get_weight, get_readout):
        own.start()

    greet(((1, Z, zpeer), (1, Y, ypeer), (1, PP, ppeer)))


    def k_send(d):
        to = rem(z + d, Z)
        return send(lanes(keys, to, HD), r.kz.at[seq], r.ks.at[d], r.kr.at[d], to * Y + y, dp)

    def h_send(d):
        to = rem(dp + d, PP)
        return send(lanes(hidden, to, feat), r.cols.at[slot], r.hs.at[d], r.hr.at[d], seq, to)

    def q_send(d):
        to = rem(z + d, Z)
        return send(lanes(queries, to, qw), r.qz.at[z], r.qs.at[d], r.qr.at[d], to * Y + y, dp)

    loop(1, Z, lambda d: k_send(d).start())
    loop(1, PP, lambda d: h_send(d).start())
    q_first = min(Z, 5)
    q_second = max(q_first, Z - 1)
    loop(1, q_first, lambda m: q_send(near(m)).start())

    def forward(ref, first, d, e, ssem, rsem):
        at = rem(z - d + Z, Z) * Y + y
        src = first if first is not None else ref.at[at]
        return send(src, ref.at[at], ssem.at[d, e], rsem.at[d, e], *ypeer(e))

    def k_forward(first, d, e):
        return forward(r.kz, first, d, e, r.kys, r.kyr)

    def v_forward(first, d, e):
        return forward(r.vz, first, d, e, r.vys, r.vyr)

    def v_send(d):
        return send(r.val.at[d], r.vz.at[seq], r.vs.at[d], r.vr.at[d], *zpeer(d))

    def pass_on(sent, via, d):
        sent(d).wait_recv()
        loop(1, Y, lambda e: via(None, d, e).start())

    k_mine = lanes(keys, z, HD)
    v_mine = r.val.at[Z]
    loop(1, Y, lambda e: k_forward(k_mine, 0, e).start())
    loop(1, Z, lambda d: pass_on(k_send, k_forward, d))


    get_weight.wait()
    own_h.wait()
    loop(1, PP, lambda d: h_send(d).wait_recv())
    half = X * TOK
    other = 1 - c

    def c_send(i):
        src = r.part.at[i, aligned(other * half, half)]
        return send(src, r.pair.at[i], r.cs.at[i], r.cr.at[i], seq, sibling)

    def product(i):
        head = rem(z + i, Z)
        block = r.cols[...].reshape(PP * TOK, feat)
        r.part[i] = jnp.dot(
            block, r.weight[:, aligned(head * HD, HD)], preferred_element_type=F32
        ).astype(BF16)
        c_send(i).start()

    loop(q_first, q_second, lambda m: q_send(near(m)).start())
    loop(1, Z + 1, product)

    def x_send(i, d):
        to = rem(x + d, X)
        src = r.both.at[i, aligned(to * TOK, TOK)]
        return send(src, r.xin.at[i, d], r.xs.at[i, d], r.xr.at[i, d], seq, to * C + c)

    def join(i):
        c_send(i).wait_recv()
        mine = r.part[i, aligned(c * half, half)].astype(F32)
        r.both[i] = (mine + r.pair[i].astype(F32)).astype(BF16)
        loop(1, X, lambda d: x_send(i, d).start())

    def values_out(i):
        total = r.both[i, aligned(x * TOK, TOK)].astype(F32)
        for d in range(1, X):
            x_send(i, d).wait_recv()
            total = total + r.xin[i, d].astype(F32)
        block = total.astype(BF16)
        r.val[i] = block

        @pl.when(i < Z)
        def _():
            v_send(i).start()

        @pl.when(i == Z)
        def _():
            r.vz[seq] = block

    def values_on(i):
        @pl.when(i < Z)
        def _():
            pass_on(v_send, v_forward, i)

        @pl.when(i == Z)
        def _():
            loop(1, Y, lambda e: v_forward(v_mine, i, e).start())


    own_k.wait()
    own_q.wait()
    loop(1, Y, lambda e: k_forward(k_mine, 0, e).wait_recv())
    loop(1, Z, lambda d: loop(1, Y, lambda e: k_forward(None, d, e).wait_recv()))
    factor = math.log2(math.e) / math.sqrt(HD)

    def fold(a, op):
        return op(a.reshape(chunk // 8, 8, wide), axis=0)

    def keys_of(j):
        return r.kz[pl.ds(j * Y, Y)].reshape(chunk, HD)

    def weights_of(t):
        q_block = r.qz[t]
        q_rows = jnp.concatenate([q_block[:, h * HD : (h + 1) * HD] for h in range(group)], axis=0)
        at = t * (t + 1) // 2

        def first(j, peak):
            s = contract(keys_of(j), q_rows, 1, 1)
            r.raw[aligned(j * chunk, chunk), :] = s
            return jnp.maximum(peak, fold(s, jnp.max))

        s = contract(keys_of(t), q_rows, 1, 1)
        key_at = lax.broadcasted_iota(jnp.int32, (chunk, wide), 0)
        query_at = lax.broadcasted_iota(jnp.int32, (chunk, wide), 1)
        s = jnp.where(key_at <= (query_at & (TOK - 1)) + y * TOK, s, SMALL)
        r.raw[aligned(t * chunk, chunk), :] = s
        peak = lax.fori_loop(0, t, first, fold(s, jnp.max))
        peak = jnp.max(peak, axis=0, keepdims=True)

        def second(j, total):
            e = jnp.exp2((r.raw[aligned(j * chunk, chunk), :] - peak) * factor)
            r.kept[at + j] = e.astype(BF16)
            return total + fold(e, jnp.sum)

        total = lax.fori_loop(0, t + 1, second, jnp.zeros((8, wide), F32))
        scale = 1.0 / jnp.sum(total, axis=0, keepdims=True)
        r.inverse[t] = jnp.broadcast_to(scale, (8, wide))

    values_stages = (join, values_out, values_on)

    def front_tick(m):
        for at, stage in enumerate(values_stages):

            @pl.when((m >= at) & (m - at < Z // 2))
            def _(at=at, stage=stage):
                stage(2 * (m - at) + 1)
                stage(2 * (m - at) + 2)

        @pl.when(m == Z // 2)
        def _():
            loop(q_second, Z, lambda i: q_send(near(i)).start())

        @pl.when(m < Z)
        def _():
            score_step(m)

    def score_step(m):
        d = near(m)

        @pl.when(d > 0)
        def _():
            q_send(d).wait_recv()

        weights_of(rem(z - d + Z, Z))

    late = Z // 2 + len(values_stages) - 1
    loop(0, late, front_tick)


    def drain_front():
        loop(1, Y, lambda e: k_forward(k_mine, 0, e).wait_send())
        loop(1, Y, lambda e: v_forward(v_mine, Z, e).wait_send())
        loop(1, PP, lambda d: h_send(d).wait_send())

        def both_ways(i):
            c_send(i).wait_send()
            loop(1, X, lambda d: x_send(i, d).wait_send())

        loop(1, Z + 1, both_ways)

        def one(i):
            loop(1, Y, lambda e: k_forward(None, i, e).wait_send())
            loop(1, Y, lambda e: v_forward(None, i, e).wait_send())
            for sent in (k_send, q_send, v_send):
                sent(i).wait_send()

        loop(1, Z, one)


    get_readout.wait()
    loop(1, Y, lambda e: v_forward(v_mine, Z, e).wait_recv())
    loop(1, Z, lambda d: loop(1, Y, lambda e: v_forward(None, d, e).wait_recv()))

    def turn(j):
        r.vt[j] = r.vz[pl.ds(j * Y, Y)].reshape(chunk, HD).astype(F32).T.astype(BF16)

    loop(0, Z, turn)

    def l_send(d):
        to = rem(z + d, Z)
        return send(r.share.at[to], r.arrived.at[d], r.ls.at[d], r.lr.at[d], to * Y + y, dp)

    def share_step(i):
        behind = late + i // 2 - 1

        @pl.when((rem(i, 2) == 1) & (i > 1) & (behind < Z))
        def _():
            score_step(behind)

        d = near(rem(i, Z))
        t = rem(z - d + Z, Z)
        at = t * (t + 1) // 2
        r.out[...] = jnp.zeros_like(r.out)

        def add(j):
            r.out[...] += jnp.dot(r.vt[j], r.kept[at + j], preferred_element_type=F32)

        loop(0, t + 1, add)
        mixed = (r.out[...] * r.inverse[t][:1]).astype(BF16)
        part = jnp.zeros((TOK, r.readout.shape[1]), F32)
        for h in range(group):
            at = slice(h * HD, (h + 1) * HD)
            part = part + contract(mixed[:, at], r.readout[at, :], 0, 0)
        r.share[t] = part.astype(BF16)

        @pl.when(d > 0)
        def _():
            l_send(Z - d).start()

    loop(1, Z + 1, share_step)

    def clear(j):
        r.total[j] = jnp.zeros((chunk, HD), F32)

    loop(0, Z, clear)
    total = base[...] + r.share[z].astype(F32)
    for d in range(1, Z):
        l_send(d).wait_recv()
        total = total + r.arrived[d].astype(F32)
    peak = jnp.max(total, axis=1, keepdims=True)
    e = jnp.exp(total - peak)
    soft = e / jnp.sum(e, axis=1, keepdims=True)
    label = jnp.broadcast_to(labels[...].astype(F32), (8, TOK)).T[:, :1]
    column = lax.broadcasted_iota(jnp.int32, total.shape, 1).astype(F32)
    r.slopes[z] = (soft - jnp.where(label == column, 1.0, 0.0)).astype(BF16)

    def s_send(d):
        return send(r.slopes.at[z], r.slopes.at[z], r.ss.at[d], r.sr.at[d], *zpeer(d))

    loop(1, Z, lambda m: s_send(near(m)).start())

    def slope_step(m):
        d = near(m)

        @pl.when(d > 0)
        def _():
            s_send(d).wait_recv()

        t = rem(z - d + Z, Z)
        slope = r.slopes[t]
        for h in range(group):
            at = slice(h * HD, (h + 1) * HD)
            column = r.inverse[t][:, at].T[:, :1]
            r.d_rows[at, :] = (contract(slope, r.readout[at, :], 1, 1) * column).astype(BF16)

        def add(j):
            r.total[j] += jnp.dot(
                r.kept[t * (t + 1) // 2 + j], r.d_rows[...], preferred_element_type=F32
            )

        loop(0, t + 1, add)

    loop(0, Z, slope_step)

    def drain_middle():
        def one(i):
            l_send(i).wait_send()
            s_send(i).wait_send()

        loop(1, Z, one)


    tokens = PP * TOK
    quarter = HD // Y

    def head_lanes(ref, h):
        return ref.at[:, aligned(h * HD, HD)]

    def y1(i, e):
        to = rem(y + e, Y)
        return send(r.grads.at[i, to], r.ya.at[i, e], r.y1s.at[i, e], r.y1r.at[i, e], *ypeer(e))

    def stage0(i):
        j = rem(z + i, Z)
        for b in range(Y):
            r.grads[i, b] = r.total[j, b * TOK : (b + 1) * TOK, :].astype(BF16)
        loop(1, Y, lambda e: y1(i, e).start())

    def z1(i):
        to = rem(z + i, Z)
        dst = head_lanes(r.dv.at[slot], z)
        return send(r.dz.at[i], dst, r.z1s.at[i], r.z1r.at[i], to * Y + y, dp)

    own_dv = pltpu.make_async_copy(r.dz.at[Z], head_lanes(r.dv.at[slot], z), r.loc.at[6])

    def stage1(i):
        loop(1, Y, lambda e: y1(i, e).wait_recv())
        block = r.grads[i, y].astype(F32)
        for e in range(1, Y):
            block = block + r.ya[i, e].astype(F32)
        r.dz[i] = block.astype(BF16)

        @pl.when(i < Z)
        def _():
            z1(i).start()

        @pl.when(i == Z)
        def _():
            own_dv.start()

    def head_at(i):
        return rem(z - i + Z, Z)

    def xx(i, d):
        ref = head_lanes(r.dv.at[slot], head_at(i))
        return send(ref, ref, r.x2s.at[i, d], r.x2r.at[i, d], *xpeer(d))

    def cc(i, d):
        at = c * X + rem(x - d + X, X)
        ref = head_lanes(r.dv.at[at], head_at(i))
        return send(ref, ref, r.c2s.at[i, d], r.c2r.at[i, d], seq, sibling)

    def stage2(i):
        @pl.when(i < Z)
        def _():
            z1(i).wait_recv()

        @pl.when(i == Z)
        def _():
            own_dv.wait()

        loop(1, X, lambda d: xx(i, d).start())
        cc(i, 0).start()

    def stage3(i):
        def on(d):
            xx(i, d).wait_recv()
            cc(i, d).start()

        loop(1, X, on)

    def y2(i, e):
        to = rem(y + e, Y)
        return send(r.gp.at[i, to], r.gy.at[i, e], r.y2s.at[i, e], r.y2r.at[i, e], *ypeer(e))

    def stage4(i):
        loop(0, X, lambda d: cc(i, d).wait_recv())
        left = r.dv[:, :, aligned(head_at(i) * HD, HD)].reshape(tokens, HD)
        right = r.cols[...].reshape(tokens, feat)
        r.gp[i] = contract(left, right, 0, 0).astype(BF16).reshape(Y, quarter, feat)
        loop(1, Y, lambda e: y2(i, e).start())

    def z2(i):
        return send(r.gz.at[i], r.gr.at[i], r.z2s.at[i], r.z2r.at[i], head_at(i) * Y + y, dp)

    def stage5(i):
        loop(1, Y, lambda e: y2(i, e).wait_recv())
        block = r.gp[i, y].astype(F32)
        for e in range(1, Y):
            block = block + r.gy[i, e].astype(F32)

        @pl.when(i < Z)
        def _():
            r.gz[i] = block.astype(BF16)
            z2(i).start()

        @pl.when(i == Z)
        def _():
            r.own[...] = block

    r.sum[...] = jnp.zeros_like(r.sum)

    def stage6(i):
        @pl.when(i < Z)
        def _():
            z2(i).wait_recv()
            r.sum[...] += r.gr[i].astype(F32)

    def drain_last():
        def one(i):
            z1(i).wait_send()
            z2(i).wait_send()

        loop(1, Z, one)

        def more(i):
            loop(1, Y, lambda e: y1(i, e).wait_send())
            loop(1, Y, lambda e: y2(i, e).wait_send())
            loop(1, X, lambda d: xx(i, d).wait_send())
            loop(0, X, lambda d: cc(i, d).wait_send())

        loop(1, Z + 1, more)

    stages = (
        (14, stage6),
        (11, stage5),
        (8, stage4),
        (6, stage3),
        (3, stage2),
        (0, stage1),
    )
    loop(1, Z + 1, stage0)

    def tick(k):
        for late, stage in stages:

            @pl.when((k - late >= 1) & (k - late <= Z))
            def _(late=late, stage=stage):
                stage(k - late)

    loop(1, Z + 1 + stages[0][0], tick)
    result[...] = r.sum[...] + r.own[...]

    drain_front()
    drain_middle()
    drain_last()


def whole(n, hidden, queries, keys, weight, readout, base, labels, rows):
    Z, Y, X, PP = n.Z, n.Y, n.X, n.P
    feat = hidden.shape[1] // PP
    qw = queries.shape[1] // Z
    kv = keys.shape[1]
    cand = readout.shape[1]
    chunk = Y * TOK
    dma = pltpu.SemaphoreType.DMA
    vmem = pltpu.VMEM
    scratch = dict(
        weight=vmem((feat, kv), BF16),
        readout=vmem((qw, cand), BF16),
        cols=vmem((PP, TOK, feat), BF16),
        qz=vmem((Z, TOK, qw), BF16),
        kz=vmem((n.S, TOK, HD), BF16),
        vz=vmem((n.S, TOK, HD), BF16),
        part=vmem((Z + 1, PP * TOK, HD), BF16),
        pair=vmem((Z + 1, X * TOK, HD), BF16),
        both=vmem((Z + 1, X * TOK, HD), BF16),
        xin=vmem((Z + 1, X, TOK, HD), BF16),
        val=vmem((Z + 1, TOK, HD), BF16),
        raw=vmem((Z * chunk, qw), F32),
        vt=vmem((Z, HD, chunk), BF16),
        out=vmem((HD, qw), F32),
        kept=vmem((Z * (Z + 1) // 2, chunk, qw), BF16),
        inverse=vmem((Z, 8, qw), F32),
        share=vmem((Z, TOK, cand), BF16),
        arrived=vmem((Z, TOK, cand), BF16),
        slopes=vmem((Z, TOK, cand), BF16),
        d_rows=vmem((qw, HD), BF16),
        total=vmem((Z, chunk, HD), F32),
        grads=vmem((Z + 1, Y, TOK, HD), BF16),
        ya=vmem((Z + 1, Y, TOK, HD), BF16),
        dz=vmem((Z + 1, TOK, HD), BF16),
        dv=vmem((PP, TOK, kv), BF16),
        gp=vmem((Z + 1, Y, rows, feat), BF16),
        gy=vmem((Z + 1, Y, rows, feat), BF16),
        gz=vmem((Z, rows, feat), BF16),
        gr=vmem((Z, rows, feat), BF16),
        sum=vmem((rows, feat), F32),
        own=vmem((rows, feat), F32),
        loc=dma((7,)),
    )
    for name in ("h",):
        scratch |= {name + "s": dma((PP,)), name + "r": dma((PP,))}
    for name in ("k", "q", "v", "l", "s", "z1", "z2"):
        scratch |= {name + "s": dma((Z,)), name + "r": dma((Z,))}
    scratch |= {"cs": dma((Z + 1,)), "cr": dma((Z + 1,))}
    for name in ("ky", "vy", "y1", "y2"):
        scratch |= {name + "s": dma((Z + 1, Y)), name + "r": dma((Z + 1, Y))}
    for name in ("x", "x2", "c2"):
        scratch |= {name + "s": dma((Z + 1, X)), name + "r": dma((Z + 1, X))}
    return pl.pallas_call(
        functools.partial(whole_kernel, n, tuple(scratch)),
        out_shape=jax.ShapeDtypeStruct((rows, feat), F32),
        in_specs=[ANY, ANY, ANY, ANY, ANY, VMEM, VMEM],
        out_specs=VMEM,
        scratch_shapes=list(scratch.values()),
        compiler_params=pltpu.CompilerParams(
            collective_id=0, has_side_effects=True, vmem_limit_bytes=64 * 1024 * 1000
        ),
        name="whole",
    )(hidden, queries, keys, weight, readout, base, labels)


def local(queries, keys, hidden, value_weight, readout, base_logits, labels, hessian):
    n = sizes_of(lax.axis_size("seq"), lax.axis_size("dp"))
    total = whole(
        n,
        hidden[0],
        queries[0],
        keys[0],
        value_weight,
        readout,
        base_logits[0],
        labels,
        hessian.shape[0],
    )
    estimate = total * total / (n.S * TOK * n.P)
    return estimate, beta_two * hessian + (1.0 - beta_two) * estimate


def solution(mesh):
    placed = (
        P("dp", "seq", None),
        P("dp", "seq", None),
        P("dp", "seq", None),
        P("dp", None),
        P(),
        P("dp", "seq", None),
        P("dp", "seq"),
        P("seq", "dp"),
    )
    return jax.shard_map(
        local,
        mesh=mesh,
        in_specs=placed,
        out_specs=(P("seq", "dp"), P("seq", "dp")),
        check_vma=False,
    )
```

```python
import functools
import math
import types

import jax
import jax.numpy as jnp
from jax import lax
from jax.experimental import pallas as pl
from jax.experimental.pallas import tpu as pltpu
from jax.sharding import PartitionSpec as P

HD = 128
TOK = 128
SMALL = -1.0e30
beta_two = 0.99
MESH = pl.DeviceIdType.MESH
F32 = jnp.float32
BF16 = jnp.bfloat16
VMEM = pl.BlockSpec(memory_space=pltpu.VMEM)
ANY = pl.BlockSpec(memory_space=pl.ANY)


def sizes_of(seq, dp):
    n = types.SimpleNamespace(S=seq, P=dp, C=2, X=dp // 2)
    n.Y = 4 if seq == 32 else 2
    n.Z = seq // n.Y
    return n


def place():
    return lax.axis_index("seq"), lax.axis_index("dp")


def rem(a, b):
    return lax.rem(a, jnp.int32(b))


def loop(low, high, step):
    def body(i, carry):
        step(i)
        return carry

    lax.fori_loop(low, high, body, 0)


def aligned(start, size):
    return pl.ds(pl.multiple_of(start, size), size)


def send(src, dst, send_sem, recv_sem, seq, dp):
    return pltpu.make_async_remote_copy(
        src_ref=src,
        dst_ref=dst,
        send_sem=send_sem,
        recv_sem=recv_sem,
        device_id=(seq, dp),
        device_id_type=MESH,
    )


def greet(peers):
    barrier = pltpu.get_barrier_semaphore()
    count = 0
    for low, high, where in peers:

        def one(d, where=where):
            seq, dp = where(d)
            pl.semaphore_signal(barrier, inc=1, device_id=(seq, dp), device_id_type=MESH)

        loop(low, high, one)
        count += high - low
    pl.semaphore_wait(barrier, count)


def contract(a, b, da, db):
    return lax.dot_general(a, b, (((da,), (db,)), ((), ())), preferred_element_type=F32)


def whole_kernel(n, names, hidden, queries, keys, weight_in, readout_in, base, labels, result, *scratch):
    r = types.SimpleNamespace(**dict(zip(names, scratch, strict=True)))
    seq, dp = place()
    Z, Y, X, C, PP = n.Z, n.Y, n.X, n.C, n.P
    z, y = seq // Y, rem(seq, Y)
    x, c = dp // C, rem(dp, C)
    feat = hidden.shape[1] // PP
    qw = queries.shape[1] // Z
    kv = keys.shape[1]
    group = qw // HD
    chunk = Y * TOK
    wide = group * TOK
    sibling = x * C + 1 - c
    slot = c * X + x

    def zpeer(d):
        return rem(z + d, Z) * Y + y, dp

    def ypeer(e):
        return z * Y + rem(y + e, Y), dp

    def ppeer(d):
        return seq, rem(dp + d, PP)

    def xpeer(d):
        return seq, rem(x + d, X) * C + c

    def near(m):
        odd = rem(m, 2)
        return odd * ((m + 1) // 2) + (1 - odd) * rem(Z - m // 2, Z)

    def lanes(ref, i, width):
        return ref.at[:, aligned(i * width, width)]

    get_weight = pltpu.make_async_copy(weight_in, r.weight, r.loc.at[4])
    get_readout = pltpu.make_async_copy(readout_in.at[aligned(z * qw, qw)], r.readout, r.loc.at[5])
    own_k = pltpu.make_async_copy(lanes(keys, z, HD), r.kz.at[seq], r.loc.at[0])
    own_h = pltpu.make_async_copy(lanes(hidden, dp, feat), r.cols.at[slot], r.loc.at[1])
    own_q = pltpu.make_async_copy(lanes(queries, z, qw), r.qz.at[z], r.loc.at[2])
    for own in (own_k, own_h, own_q, get_weight, get_readout):
        own.start()

    greet(((1, Z, zpeer), (1, Y, ypeer), (1, PP, ppeer)))


    def k_send(d):
        to = rem(z + d, Z)
        return send(lanes(keys, to, HD), r.kz.at[seq], r.ks.at[d], r.kr.at[d], to * Y + y, dp)

    def h_send(d):
        to = rem(dp + d, PP)
        return send(lanes(hidden, to, feat), r.cols.at[slot], r.hs.at[d], r.hr.at[d], seq, to)

    def q_send(d):
        to = rem(z + d, Z)
        return send(lanes(queries, to, qw), r.qz.at[z], r.qs.at[d], r.qr.at[d], to * Y + y, dp)

    loop(1, Z, lambda d: k_send(d).start())
    loop(1, PP, lambda d: h_send(d).start())
    q_first = min(Z, 5)
    q_second = max(q_first, Z - 1)
    loop(1, q_first, lambda m: q_send(near(m)).start())

    def forward(ref, first, d, e, ssem, rsem):
        at = rem(z - d + Z, Z) * Y + y
        src = first if first is not None else ref.at[at]
        return send(src, ref.at[at], ssem.at[d, e], rsem.at[d, e], *ypeer(e))

    def k_forward(first, d, e):
        return forward(r.kz, first, d, e, r.kys, r.kyr)

    def v_forward(first, d, e):
        return forward(r.vz, first, d, e, r.vys, r.vyr)

    def v_send(d):
        return send(r.val.at[d], r.vz.at[seq], r.vs.at[d], r.vr.at[d], *zpeer(d))

    def pass_on(sent, via, d):
        sent(d).wait_recv()
        loop(1, Y, lambda e: via(None, d, e).start())

    k_mine = lanes(keys, z, HD)
    v_mine = r.val.at[Z]
    loop(1, Y, lambda e: k_forward(k_mine, 0, e).start())
    loop(1, Z, lambda d: pass_on(k_send, k_forward, d))


    get_weight.wait()
    own_h.wait()
    loop(1, PP, lambda d: h_send(d).wait_recv())
    half = X * TOK
    other = 1 - c

    def c_send(i):
        src = r.part.at[i, aligned(other * half, half)]
        return send(src, r.pair.at[i], r.cs.at[i], r.cr.at[i], seq, sibling)

    def product(i):
        head = rem(z + i, Z)
        block = r.cols[...].reshape(PP * TOK, feat)
        r.part[i] = jnp.dot(
            block, r.weight[:, aligned(head * HD, HD)], preferred_element_type=F32
        ).astype(BF16)
        c_send(i).start()

    loop(q_first, q_second, lambda m: q_send(near(m)).start())
    loop(1, Z + 1, product)

    def x_send(i, d):
        to = rem(x + d, X)
        src = r.both.at[i, aligned(to * TOK, TOK)]
        return send(src, r.xin.at[i, d], r.xs.at[i, d], r.xr.at[i, d], seq, to * C + c)

    def join(i):
        c_send(i).wait_recv()
        mine = r.part[i, aligned(c * half, half)].astype(F32)
        r.both[i] = (mine + r.pair[i].astype(F32)).astype(BF16)
        loop(1, X, lambda d: x_send(i, d).start())

    def values_out(i):
        total = r.both[i, aligned(x * TOK, TOK)].astype(F32)
        for d in range(1, X):
            x_send(i, d).wait_recv()
            total = total + r.xin[i, d].astype(F32)
        block = total.astype(BF16)
        r.val[i] = block

        @pl.when(i < Z)
        def _():
            v_send(i).start()

        @pl.when(i == Z)
        def _():
            r.vz[seq] = block

    def values_on(i):
        @pl.when(i < Z)
        def _():
            pass_on(v_send, v_forward, i)

        @pl.when(i == Z)
        def _():
            loop(1, Y, lambda e: v_forward(v_mine, i, e).start())

    loop(1, Z + 1, join)


    own_k.wait()
    own_q.wait()
    loop(1, Y, lambda e: k_forward(k_mine, 0, e).wait_recv())
    loop(1, Z, lambda d: loop(1, Y, lambda e: k_forward(None, d, e).wait_recv()))
    factor = math.log2(math.e) / math.sqrt(HD)

    def fold(a, op):
        return op(a.reshape(chunk // 8, 8, wide), axis=0)

    def keys_of(j):
        return r.kz[pl.ds(j * Y, Y)].reshape(chunk, HD)

    def weights_of(t):
        q_block = r.qz[t]
        q_rows = jnp.concatenate([q_block[:, h * HD : (h + 1) * HD] for h in range(group)], axis=0)
        at = t * (t + 1) // 2

        def first(j, peak):
            s = contract(keys_of(j), q_rows, 1, 1)
            r.raw[aligned(j * chunk, chunk), :] = s
            return jnp.maximum(peak, fold(s, jnp.max))

        s = contract(keys_of(t), q_rows, 1, 1)
        key_at = lax.broadcasted_iota(jnp.int32, (chunk, wide), 0)
        query_at = lax.broadcasted_iota(jnp.int32, (chunk, wide), 1)
        s = jnp.where(key_at <= (query_at & (TOK - 1)) + y * TOK, s, SMALL)
        r.raw[aligned(t * chunk, chunk), :] = s
        peak = lax.fori_loop(0, t, first, fold(s, jnp.max))
        peak = jnp.max(peak, axis=0, keepdims=True)

        def second(j, total):
            e = jnp.exp2((r.raw[aligned(j * chunk, chunk), :] - peak) * factor)
            r.kept[at + j] = e.astype(BF16)
            return total + fold(e, jnp.sum)

        total = lax.fori_loop(0, t + 1, second, jnp.zeros((8, wide), F32))
        scale = 1.0 / jnp.sum(total, axis=0, keepdims=True)
        r.inverse[t] = jnp.broadcast_to(scale, (8, wide))

    values_stages = ((1, values_out), (3, values_on))

    def front_tick(m):
        for at, stage in values_stages:

            @pl.when((m >= at) & (m - at < Z // 2))
            def _(at=at, stage=stage):
                stage(2 * (m - at) + 1)
                stage(2 * (m - at) + 2)

        @pl.when(m == Z // 2)
        def _():
            loop(q_second, Z, lambda i: q_send(near(i)).start())

        @pl.when(m < Z)
        def _():
            score_step(m)

    def score_step(m):
        d = near(m)

        @pl.when(d > 0)
        def _():
            q_send(d).wait_recv()

        weights_of(rem(z - d + Z, Z))

    loop(0, max(Z, Z // 2 + values_stages[-1][0]), front_tick)


    def drain_front():
        loop(1, Y, lambda e: k_forward(k_mine, 0, e).wait_send())
        loop(1, Y, lambda e: v_forward(v_mine, Z, e).wait_send())
        loop(1, PP, lambda d: h_send(d).wait_send())

        def both_ways(i):
            c_send(i).wait_send()
            loop(1, X, lambda d: x_send(i, d).wait_send())

        loop(1, Z + 1, both_ways)

        def one(i):
            loop(1, Y, lambda e: k_forward(None, i, e).wait_send())
            loop(1, Y, lambda e: v_forward(None, i, e).wait_send())
            for sent in (k_send, q_send, v_send):
                sent(i).wait_send()

        loop(1, Z, one)


    get_readout.wait()
    loop(1, Y, lambda e: v_forward(v_mine, Z, e).wait_recv())
    loop(1, Z, lambda d: loop(1, Y, lambda e: v_forward(None, d, e).wait_recv()))

    def turn(j):
        r.vt[j] = r.vz[pl.ds(j * Y, Y)].reshape(chunk, HD).astype(F32).T.astype(BF16)

    loop(0, Z, turn)

    def l_send(d):
        to = rem(z + d, Z)
        return send(r.share.at[to], r.arrived.at[d], r.ls.at[d], r.lr.at[d], to * Y + y, dp)

    def share_step(i):
        d = near(Z - i)
        t = rem(z - d + Z, Z)
        at = t * (t + 1) // 2
        r.out[...] = jnp.zeros_like(r.out)

        def add(j):
            r.out[...] += jnp.dot(r.vt[j], r.kept[at + j], preferred_element_type=F32)

        loop(0, t + 1, add)
        mixed = (r.out[...] * r.inverse[t][:1]).astype(BF16)
        part = jnp.zeros((TOK, r.readout.shape[1]), F32)
        for h in range(group):
            at = slice(h * HD, (h + 1) * HD)
            part = part + contract(mixed[:, at], r.readout[at, :], 0, 0)
        r.share[t] = part.astype(BF16)

        @pl.when(d > 0)
        def _():
            l_send(Z - d).start()

    loop(1, Z + 1, share_step)

    def clear(j):
        r.total[j] = jnp.zeros((HD, chunk), F32)

    loop(0, Z, clear)
    total = base[...] + r.share[z].astype(F32)
    for d in range(1, Z):
        l_send(d).wait_recv()
        total = total + r.arrived[d].astype(F32)
    peak = jnp.max(total, axis=1, keepdims=True)
    e = jnp.exp(total - peak)
    soft = e / jnp.sum(e, axis=1, keepdims=True)
    label = jnp.broadcast_to(labels[...].astype(F32), (8, TOK)).T[:, :1]
    column = lax.broadcasted_iota(jnp.int32, total.shape, 1).astype(F32)
    r.slopes[z] = (soft - jnp.where(label == column, 1.0, 0.0)).astype(BF16)

    def s_send(d):
        return send(r.slopes.at[z], r.slopes.at[z], r.ss.at[d], r.sr.at[d], *zpeer(d))

    loop(1, Z, lambda m: s_send(near(m)).start())

    def slope_step(m):
        d = near(m)

        @pl.when(d > 0)
        def _():
            s_send(d).wait_recv()

        t = rem(z - d + Z, Z)
        slope = r.slopes[t]
        for h in range(group):
            at = slice(h * HD, (h + 1) * HD)
            d_head = contract(r.readout[at, :], slope, 1, 1)
            r.d_rows[:, at] = (d_head * r.inverse[t][:1, at]).astype(BF16)

        def add(j):
            r.total[j] += contract(r.d_rows[...], r.kept[t * (t + 1) // 2 + j], 1, 1)

        loop(0, t + 1, add)

    loop(0, Z, slope_step)

    def drain_middle():
        def one(i):
            l_send(i).wait_send()
            s_send(i).wait_send()

        loop(1, Z, one)


    tokens = PP * TOK
    quarter = HD // Y

    def head_lanes(ref, h):
        return ref.at[:, aligned(h * HD, HD)]

    def y1(i, e):
        to = rem(y + e, Y)
        return send(r.grads.at[i, to], r.ya.at[i, e], r.y1s.at[i, e], r.y1r.at[i, e], *ypeer(e))

    def stage0(i):
        j = rem(z + i, Z)
        for b in range(Y):
            r.grads[i, b] = r.total[j, :, b * TOK : (b + 1) * TOK].T.astype(BF16)
        loop(1, Y, lambda e: y1(i, e).start())

    def z1(i):
        to = rem(z + i, Z)
        dst = head_lanes(r.dv.at[slot], z)
        return send(r.dz.at[i], dst, r.z1s.at[i], r.z1r.at[i], to * Y + y, dp)

    own_dv = pltpu.make_async_copy(r.dz.at[Z], head_lanes(r.dv.at[slot], z), r.loc.at[6])

    def stage1(i):
        loop(1, Y, lambda e: y1(i, e).wait_recv())
        block = r.grads[i, y].astype(F32)
        for e in range(1, Y):
            block = block + r.ya[i, e].astype(F32)
        r.dz[i] = block.astype(BF16)

        @pl.when(i < Z)
        def _():
            z1(i).start()

        @pl.when(i == Z)
        def _():
            own_dv.start()

    def head_at(i):
        return rem(z - i + Z, Z)

    def xx(i, d):
        ref = head_lanes(r.dv.at[slot], head_at(i))
        return send(ref, ref, r.x2s.at[i, d], r.x2r.at[i, d], *xpeer(d))

    def cc(i, d):
        at = c * X + rem(x - d + X, X)
        ref = head_lanes(r.dv.at[at], head_at(i))
        return send(ref, ref, r.c2s.at[i, d], r.c2r.at[i, d], seq, sibling)

    def stage2(i):
        @pl.when(i < Z)
        def _():
            z1(i).wait_recv()

        @pl.when(i == Z)
        def _():
            own_dv.wait()

        loop(1, X, lambda d: xx(i, d).start())
        cc(i, 0).start()

    def stage3(i):
        def on(d):
            xx(i, d).wait_recv()
            cc(i, d).start()

        loop(1, X, on)

    def y2(i, e):
        to = rem(y + e, Y)
        return send(r.gp.at[i, to], r.gy.at[i, e], r.y2s.at[i, e], r.y2r.at[i, e], *ypeer(e))

    def stage4(i):
        loop(0, X, lambda d: cc(i, d).wait_recv())
        left = r.dv[:, :, aligned(head_at(i) * HD, HD)].reshape(tokens, HD)
        right = r.cols[...].reshape(tokens, feat)
        r.gp[i] = contract(left, right, 0, 0).astype(BF16).reshape(Y, quarter, feat)
        loop(1, Y, lambda e: y2(i, e).start())

    def z2(i):
        return send(r.gz.at[i], r.gr.at[i], r.z2s.at[i], r.z2r.at[i], head_at(i) * Y + y, dp)

    def stage5(i):
        loop(1, Y, lambda e: y2(i, e).wait_recv())
        block = r.gp[i, y].astype(F32)
        for e in range(1, Y):
            block = block + r.gy[i, e].astype(F32)

        @pl.when(i < Z)
        def _():
            r.gz[i] = block.astype(BF16)
            z2(i).start()

        @pl.when(i == Z)
        def _():
            r.own[...] = block

    r.sum[...] = jnp.zeros_like(r.sum)

    def stage6(i):
        @pl.when(i < Z)
        def _():
            z2(i).wait_recv()
            r.sum[...] += r.gr[i].astype(F32)

    def drain_last():
        def one(i):
            z1(i).wait_send()
            z2(i).wait_send()

        loop(1, Z, one)

        def more(i):
            loop(1, Y, lambda e: y1(i, e).wait_send())
            loop(1, Y, lambda e: y2(i, e).wait_send())
            loop(1, X, lambda d: xx(i, d).wait_send())
            loop(0, X, lambda d: cc(i, d).wait_send())

        loop(1, Z + 1, more)

    stages = (
        (14, stage6),
        (11, stage5),
        (8, stage4),
        (6, stage3),
        (3, stage2),
        (0, stage1),
    )
    loop(1, Z + 1, stage0)

    def tick(k):
        for late, stage in stages:

            @pl.when((k - late >= 1) & (k - late <= Z))
            def _(late=late, stage=stage):
                stage(k - late)

    loop(1, Z + 1 + stages[0][0], tick)
    result[...] = r.sum[...] + r.own[...]

    drain_front()
    drain_middle()
    drain_last()


def whole(n, hidden, queries, keys, weight, readout, base, labels, rows):
    Z, Y, X, PP = n.Z, n.Y, n.X, n.P
    feat = hidden.shape[1] // PP
    qw = queries.shape[1] // Z
    kv = keys.shape[1]
    cand = readout.shape[1]
    chunk = Y * TOK
    dma = pltpu.SemaphoreType.DMA
    vmem = pltpu.VMEM
    scratch = dict(
        weight=vmem((feat, kv), BF16),
        readout=vmem((qw, cand), BF16),
        cols=vmem((PP, TOK, feat), BF16),
        qz=vmem((Z, TOK, qw), BF16),
        kz=vmem((n.S, TOK, HD), BF16),
        vz=vmem((n.S, TOK, HD), BF16),
        part=vmem((Z + 1, PP * TOK, HD), BF16),
        pair=vmem((Z + 1, X * TOK, HD), BF16),
        both=vmem((Z + 1, X * TOK, HD), BF16),
        xin=vmem((Z + 1, X, TOK, HD), BF16),
        val=vmem((Z + 1, TOK, HD), BF16),
        raw=vmem((Z * chunk, qw), F32),
        vt=vmem((Z, HD, chunk), BF16),
        out=vmem((HD, qw), F32),
        kept=vmem((Z * (Z + 1) // 2, chunk, qw), BF16),
        inverse=vmem((Z, 8, qw), F32),
        share=vmem((Z, TOK, cand), BF16),
        arrived=vmem((Z, TOK, cand), BF16),
        slopes=vmem((Z, TOK, cand), BF16),
        d_rows=vmem((HD, qw), BF16),
        total=vmem((Z, HD, chunk), F32),
        grads=vmem((Z + 1, Y, TOK, HD), BF16),
        ya=vmem((Z + 1, Y, TOK, HD), BF16),
        dz=vmem((Z + 1, TOK, HD), BF16),
        dv=vmem((PP, TOK, kv), BF16),
        gp=vmem((Z + 1, Y, rows, feat), BF16),
        gy=vmem((Z + 1, Y, rows, feat), BF16),
        gz=vmem((Z, rows, feat), BF16),
        gr=vmem((Z, rows, feat), BF16),
        sum=vmem((rows, feat), F32),
        own=vmem((rows, feat), F32),
        loc=dma((7,)),
    )
    for name in ("h",):
        scratch |= {name + "s": dma((PP,)), name + "r": dma((PP,))}
    for name in ("k", "q", "v", "l", "s", "z1", "z2"):
        scratch |= {name + "s": dma((Z,)), name + "r": dma((Z,))}
    scratch |= {"cs": dma((Z + 1,)), "cr": dma((Z + 1,))}
    for name in ("ky", "vy", "y1", "y2"):
        scratch |= {name + "s": dma((Z + 1, Y)), name + "r": dma((Z + 1, Y))}
    for name in ("x", "x2", "c2"):
        scratch |= {name + "s": dma((Z + 1, X)), name + "r": dma((Z + 1, X))}
    return pl.pallas_call(
        functools.partial(whole_kernel, n, tuple(scratch)),
        out_shape=jax.ShapeDtypeStruct((rows, feat), F32),
        in_specs=[ANY, ANY, ANY, ANY, ANY, VMEM, VMEM],
        out_specs=VMEM,
        scratch_shapes=list(scratch.values()),
        compiler_params=pltpu.CompilerParams(
            collective_id=0, has_side_effects=True, vmem_limit_bytes=64 * 1024 * 1000
        ),
        name="whole",
    )(hidden, queries, keys, weight, readout, base, labels)


def local(queries, keys, hidden, value_weight, readout, base_logits, labels, hessian):
    n = sizes_of(lax.axis_size("seq"), lax.axis_size("dp"))
    total = whole(
        n,
        hidden[0],
        queries[0],
        keys[0],
        value_weight,
        readout,
        base_logits[0],
        labels,
        hessian.shape[0],
    )
    estimate = total * total / (n.S * TOK * n.P)
    return estimate, beta_two * hessian + (1.0 - beta_two) * estimate


def solution(mesh):
    placed = (
        P("dp", "seq", None),
        P("dp", "seq", None),
        P("dp", "seq", None),
        P("dp", None),
        P(),
        P("dp", "seq", None),
        P("dp", "seq"),
        P("seq", "dp"),
    )
    return jax.shard_map(
        local,
        mesh=mesh,
        in_specs=placed,
        out_specs=(P("seq", "dp"), P("seq", "dp")),
        check_vma=False,
    )
```

```python
import functools
import math
import types

import jax
import jax.numpy as jnp
from jax import lax
from jax.experimental import pallas as pl
from jax.experimental.pallas import tpu as pltpu
from jax.sharding import PartitionSpec as P

HD = 128
TOK = 128
SMALL = -1.0e30
beta_two = 0.99
MESH = pl.DeviceIdType.MESH
F32 = jnp.float32
BF16 = jnp.bfloat16
VMEM = pl.BlockSpec(memory_space=pltpu.VMEM)
ANY = pl.BlockSpec(memory_space=pl.ANY)


def sizes_of(seq, dp):
    n = types.SimpleNamespace(S=seq, P=dp, C=2, X=dp // 2)
    n.Y = 4 if seq == 32 else 2
    n.Z = seq // n.Y
    return n


def place():
    return lax.axis_index("seq"), lax.axis_index("dp")


def rem(a, b):
    return lax.rem(a, jnp.int32(b))


def loop(low, high, step):
    def body(i, carry):
        step(i)
        return carry

    lax.fori_loop(low, high, body, 0)


def aligned(start, size):
    return pl.ds(pl.multiple_of(start, size), size)


def send(src, dst, send_sem, recv_sem, seq, dp):
    return pltpu.make_async_remote_copy(
        src_ref=src,
        dst_ref=dst,
        send_sem=send_sem,
        recv_sem=recv_sem,
        device_id=(seq, dp),
        device_id_type=MESH,
    )


def greet(peers):
    barrier = pltpu.get_barrier_semaphore()
    count = 0
    for low, high, where in peers:

        def one(d, where=where):
            seq, dp = where(d)
            pl.semaphore_signal(barrier, inc=1, device_id=(seq, dp), device_id_type=MESH)

        loop(low, high, one)
        count += high - low
    pl.semaphore_wait(barrier, count)


def contract(a, b, da, db):
    return lax.dot_general(a, b, (((da,), (db,)), ((), ())), preferred_element_type=F32)


def whole_kernel(n, names, hidden, queries, keys, weight_in, readout_in, base, labels, result, *scratch):
    r = types.SimpleNamespace(**dict(zip(names, scratch, strict=True)))
    seq, dp = place()
    Z, Y, X, C, PP = n.Z, n.Y, n.X, n.C, n.P
    z, y = seq // Y, rem(seq, Y)
    x, c = dp // C, rem(dp, C)
    feat = hidden.shape[1] // PP
    qw = queries.shape[1] // Z
    kv = keys.shape[1]
    group = qw // HD
    chunk = Y * TOK
    wide = group * TOK
    sibling = x * C + 1 - c
    slot = c * X + x

    def zpeer(d):
        return rem(z + d, Z) * Y + y, dp

    def ypeer(e):
        return z * Y + rem(y + e, Y), dp

    def ppeer(d):
        return seq, rem(dp + d, PP)

    def xpeer(d):
        return seq, rem(x + d, X) * C + c

    def near(m):
        odd = rem(m, 2)
        return odd * ((m + 1) // 2) + (1 - odd) * rem(Z - m // 2, Z)

    def lanes(ref, i, width):
        return ref.at[:, aligned(i * width, width)]

    get_weight = pltpu.make_async_copy(weight_in, r.weight, r.loc.at[4])
    get_readout = pltpu.make_async_copy(readout_in.at[aligned(z * qw, qw)], r.readout, r.loc.at[5])
    own_k = pltpu.make_async_copy(lanes(keys, z, HD), r.kz.at[seq], r.loc.at[0])
    own_h = pltpu.make_async_copy(lanes(hidden, dp, feat), r.cols.at[slot], r.loc.at[1])
    own_q = pltpu.make_async_copy(lanes(queries, z, qw), r.qz.at[z], r.loc.at[2])
    for own in (own_k, own_h, own_q, get_weight, get_readout):
        own.start()

    greet(((1, Z, zpeer), (1, Y, ypeer), (1, PP, ppeer)))


    def k_send(d):
        to = rem(z + d, Z)
        return send(lanes(keys, to, HD), r.kz.at[seq], r.ks.at[d], r.kr.at[d], to * Y + y, dp)

    def h_send(d):
        to = rem(dp + d, PP)
        return send(lanes(hidden, to, feat), r.cols.at[slot], r.hs.at[d], r.hr.at[d], seq, to)

    def q_send(d):
        to = rem(z + d, Z)
        return send(lanes(queries, to, qw), r.qz.at[z], r.qs.at[d], r.qr.at[d], to * Y + y, dp)

    loop(1, Z, lambda d: k_send(d).start())
    loop(1, PP, lambda d: h_send(d).start())
    q_first = min(Z, 5)
    q_second = max(q_first, Z - 1)
    loop(1, q_first, lambda m: q_send(near(m)).start())

    def forward(ref, first, d, e, ssem, rsem):
        at = rem(z - d + Z, Z) * Y + y
        src = first if first is not None else ref.at[at]
        return send(src, ref.at[at], ssem.at[d, e], rsem.at[d, e], *ypeer(e))

    def k_forward(first, d, e):
        return forward(r.kz, first, d, e, r.kys, r.kyr)

    def v_forward(first, d, e):
        return forward(r.vz, first, d, e, r.vys, r.vyr)

    def v_send(d):
        return send(r.val.at[d], r.vz.at[seq], r.vs.at[d], r.vr.at[d], *zpeer(d))

    def pass_on(sent, via, d):
        sent(d).wait_recv()
        loop(1, Y, lambda e: via(None, d, e).start())

    k_mine = lanes(keys, z, HD)
    v_mine = r.val.at[Z]
    loop(1, Y, lambda e: k_forward(k_mine, 0, e).start())
    loop(1, Z, lambda d: pass_on(k_send, k_forward, d))


    get_weight.wait()
    own_h.wait()
    loop(1, PP, lambda d: h_send(d).wait_recv())
    half = X * TOK
    other = 1 - c

    def c_send(i):
        src = r.part.at[i, aligned(other * half, half)]
        return send(src, r.pair.at[i], r.cs.at[i], r.cr.at[i], seq, sibling)

    def product(i):
        head = rem(z + i, Z)
        block = r.cols[...].reshape(PP * TOK, feat)
        r.part[i] = jnp.dot(
            block, r.weight[:, aligned(head * HD, HD)], preferred_element_type=F32
        ).astype(BF16)
        c_send(i).start()

    loop(q_first, q_second, lambda m: q_send(near(m)).start())
    loop(1, Z + 1, product)

    def x_send(i, d):
        to = rem(x + d, X)
        src = r.both.at[i, aligned(to * TOK, TOK)]
        return send(src, r.xin.at[i, d], r.xs.at[i, d], r.xr.at[i, d], seq, to * C + c)

    def join(i):
        c_send(i).wait_recv()
        mine = r.part[i, aligned(c * half, half)].astype(F32)
        r.both[i] = (mine + r.pair[i].astype(F32)).astype(BF16)
        loop(1, X, lambda d: x_send(i, d).start())

    def values_out(i):
        total = r.both[i, aligned(x * TOK, TOK)].astype(F32)
        for d in range(1, X):
            x_send(i, d).wait_recv()
            total = total + r.xin[i, d].astype(F32)
        block = total.astype(BF16)
        r.val[i] = block

        @pl.when(i < Z)
        def _():
            v_send(i).start()

        @pl.when(i == Z)
        def _():
            r.vz[seq] = block

    def values_on(i):
        @pl.when(i < Z)
        def _():
            pass_on(v_send, v_forward, i)

        @pl.when(i == Z)
        def _():
            loop(1, Y, lambda e: v_forward(v_mine, i, e).start())

    loop(1, Z + 1, join)


    own_k.wait()
    own_q.wait()
    loop(1, Y, lambda e: k_forward(k_mine, 0, e).wait_recv())
    loop(1, Z, lambda d: loop(1, Y, lambda e: k_forward(None, d, e).wait_recv()))
    factor = math.log2(math.e) / math.sqrt(HD)

    def fold(a, op):
        return op(a.reshape(chunk // 8, 8, wide), axis=0)

    def keys_of(j):
        return r.kz[pl.ds(j * Y, Y)].reshape(chunk, HD)

    def weights_of(t):
        q_block = r.qz[t]
        q_rows = jnp.concatenate([q_block[:, h * HD : (h + 1) * HD] for h in range(group)], axis=0)
        at = t * (t + 1) // 2

        def first(j, peak):
            s = contract(keys_of(j), q_rows, 1, 1)
            r.raw[aligned(j * chunk, chunk), :] = s
            return jnp.maximum(peak, fold(s, jnp.max))

        s = contract(keys_of(t), q_rows, 1, 1)
        key_at = lax.broadcasted_iota(jnp.int32, (chunk, wide), 0)
        query_at = lax.broadcasted_iota(jnp.int32, (chunk, wide), 1)
        s = jnp.where(key_at <= (query_at & (TOK - 1)) + y * TOK, s, SMALL)
        r.raw[aligned(t * chunk, chunk), :] = s
        peak = lax.fori_loop(0, t, first, fold(s, jnp.max))
        peak = jnp.max(peak, axis=0, keepdims=True)

        def second(j, total):
            e = jnp.exp2((r.raw[aligned(j * chunk, chunk), :] - peak) * factor)
            r.kept[at + j] = e.astype(BF16)
            return total + fold(e, jnp.sum)

        total = lax.fori_loop(0, t + 1, second, jnp.zeros((8, wide), F32))
        scale = 1.0 / jnp.sum(total, axis=0, keepdims=True)
        r.inverse[t] = jnp.broadcast_to(scale, (8, wide))

    values_stages = ((1, values_out), (3, values_on))

    def front_tick(m):
        for at, stage in values_stages:

            @pl.when((m >= at) & (m - at < Z // 2))
            def _(at=at, stage=stage):
                stage(2 * (m - at) + 1)
                stage(2 * (m - at) + 2)

        @pl.when(m == Z // 2)
        def _():
            loop(q_second, Z, lambda i: q_send(near(i)).start())

        @pl.when(m < Z)
        def _():
            score_step(m)

    def score_step(m):
        d = near(m)

        @pl.when(d > 0)
        def _():
            q_send(d).wait_recv()

        weights_of(rem(z - d + Z, Z))

    loop(0, max(Z, Z // 2 + values_stages[-1][0]), front_tick)


    def drain_front():
        loop(1, Y, lambda e: k_forward(k_mine, 0, e).wait_send())
        loop(1, Y, lambda e: v_forward(v_mine, Z, e).wait_send())
        loop(1, PP, lambda d: h_send(d).wait_send())

        def both_ways(i):
            c_send(i).wait_send()
            loop(1, X, lambda d: x_send(i, d).wait_send())

        loop(1, Z + 1, both_ways)

        def one(i):
            loop(1, Y, lambda e: k_forward(None, i, e).wait_send())
            loop(1, Y, lambda e: v_forward(None, i, e).wait_send())
            for sent in (k_send, q_send, v_send):
                sent(i).wait_send()

        loop(1, Z, one)


    get_readout.wait()
    loop(1, Y, lambda e: v_forward(v_mine, Z, e).wait_recv())
    loop(1, Z, lambda d: loop(1, Y, lambda e: v_forward(None, d, e).wait_recv()))

    def turn(j):
        r.vt[j] = r.vz[pl.ds(j * Y, Y)].reshape(chunk, HD).astype(F32).T.astype(BF16)

    loop(0, Z, turn)

    def l_send(d):
        to = rem(z + d, Z)
        return send(r.share.at[to], r.arrived.at[d], r.ls.at[d], r.lr.at[d], to * Y + y, dp)

    def share_step(i):
        d = near(Z - i)
        t = rem(z - d + Z, Z)
        at = t * (t + 1) // 2
        r.out[...] = jnp.zeros_like(r.out)

        def add(j):
            r.out[...] += jnp.dot(r.vt[j], r.kept[at + j], preferred_element_type=F32)

        loop(0, t + 1, add)
        mixed = (r.out[...] * r.inverse[t][:1]).astype(BF16)
        part = jnp.zeros((TOK, r.readout.shape[1]), F32)
        for h in range(group):
            at = slice(h * HD, (h + 1) * HD)
            part = part + contract(mixed[:, at], r.readout[at, :], 0, 0)
        r.share[t] = part.astype(BF16)

        @pl.when(d > 0)
        def _():
            l_send(Z - d).start()

    loop(1, Z + 1, share_step)

    def clear(j):
        r.total[j] = jnp.zeros((HD, chunk), F32)

    loop(0, Z, clear)
    total = base[...] + r.share[z].astype(F32)
    for d in range(1, Z):
        l_send(d).wait_recv()
        total = total + r.arrived[d].astype(F32)
    peak = jnp.max(total, axis=1, keepdims=True)
    e = jnp.exp(total - peak)
    soft = e / jnp.sum(e, axis=1, keepdims=True)
    label = jnp.broadcast_to(labels[...].astype(F32), (8, TOK)).T[:, :1]
    column = lax.broadcasted_iota(jnp.int32, total.shape, 1).astype(F32)
    r.slopes[z] = (soft - jnp.where(label == column, 1.0, 0.0)).astype(BF16)

    def s_send(d):
        up = d <= Z // 2
        at = jnp.where(up, rem(z - d + 1 + Z, Z), rem(z - d - 1 + 2 * Z, Z))
        to = jnp.where(up, rem(z + 1, Z), rem(z - 1 + Z, Z))
        ref = r.slopes.at[at]
        return send(ref, ref, r.ss.at[d], r.sr.at[d], to * Y + y, dp)

    s_send(jnp.int32(1)).start()
    if Z > 2:
        s_send(jnp.int32(Z - 1)).start()

    def slopes_on(d):
        s_send(d).wait_recv()

        @pl.when(d < Z // 2)
        def _():
            s_send(d + 1).start()

        @pl.when(d > Z // 2 + 1)
        def _():
            s_send(d - 1).start()

    def slope_step(m):
        d = near(m)

        @pl.when(rem(m, 2) == 1)
        def _():
            slopes_on(d)

            @pl.when(m + 1 < Z)
            def _():
                slopes_on(Z - d)

        t = rem(z - d + Z, Z)
        slope = r.slopes[t]
        for h in range(group):
            at = slice(h * HD, (h + 1) * HD)
            d_head = contract(r.readout[at, :], slope, 1, 1)
            r.d_rows[:, at] = (d_head * r.inverse[t][:1, at]).astype(BF16)

        def add(j):
            r.total[j] += contract(r.d_rows[...], r.kept[t * (t + 1) // 2 + j], 1, 1)

        loop(0, t + 1, add)

    loop(0, Z, slope_step)

    def drain_middle():
        def one(i):
            l_send(i).wait_send()
            s_send(i).wait_send()

        loop(1, Z, one)


    tokens = PP * TOK
    quarter = HD // Y

    def head_lanes(ref, h):
        return ref.at[:, aligned(h * HD, HD)]

    def y1(i, e):
        to = rem(y + e, Y)
        return send(r.grads.at[i, to], r.ya.at[i, e], r.y1s.at[i, e], r.y1r.at[i, e], *ypeer(e))

    def stage0(i):
        j = rem(z + i, Z)
        for b in range(Y):
            r.grads[i, b] = r.total[j, :, b * TOK : (b + 1) * TOK].T.astype(BF16)
        loop(1, Y, lambda e: y1(i, e).start())

    def z1(i):
        to = rem(z + i, Z)
        dst = head_lanes(r.dv.at[slot], z)
        return send(r.dz.at[i], dst, r.z1s.at[i], r.z1r.at[i], to * Y + y, dp)

    own_dv = pltpu.make_async_copy(r.dz.at[Z], head_lanes(r.dv.at[slot], z), r.loc.at[6])

    def stage1(i):
        loop(1, Y, lambda e: y1(i, e).wait_recv())
        block = r.grads[i, y].astype(F32)
        for e in range(1, Y):
            block = block + r.ya[i, e].astype(F32)
        r.dz[i] = block.astype(BF16)

        @pl.when(i < Z)
        def _():
            z1(i).start()

        @pl.when(i == Z)
        def _():
            own_dv.start()

    def head_at(i):
        return rem(z - i + Z, Z)

    def xx(i, d):
        ref = head_lanes(r.dv.at[slot], head_at(i))
        return send(ref, ref, r.x2s.at[i, d], r.x2r.at[i, d], *xpeer(d))

    def cc(i, d):
        at = c * X + rem(x - d + X, X)
        ref = head_lanes(r.dv.at[at], head_at(i))
        return send(ref, ref, r.c2s.at[i, d], r.c2r.at[i, d], seq, sibling)

    def stage2(i):
        @pl.when(i < Z)
        def _():
            z1(i).wait_recv()

        @pl.when(i == Z)
        def _():
            own_dv.wait()

        loop(1, X, lambda d: xx(i, d).start())
        cc(i, 0).start()

    def stage3(i):
        def on(d):
            xx(i, d).wait_recv()
            cc(i, d).start()

        loop(1, X, on)

    def y2(i, e):
        to = rem(y + e, Y)
        return send(r.gp.at[i, to], r.gy.at[i, e], r.y2s.at[i, e], r.y2r.at[i, e], *ypeer(e))

    def stage4(i):
        loop(0, X, lambda d: cc(i, d).wait_recv())
        left = r.dv[:, :, aligned(head_at(i) * HD, HD)].reshape(tokens, HD)
        right = r.cols[...].reshape(tokens, feat)
        r.gp[i] = contract(left, right, 0, 0).astype(BF16).reshape(Y, quarter, feat)
        loop(1, Y, lambda e: y2(i, e).start())

    def z2(i):
        return send(r.gz.at[i], r.gr.at[i], r.z2s.at[i], r.z2r.at[i], head_at(i) * Y + y, dp)

    def stage5(i):
        loop(1, Y, lambda e: y2(i, e).wait_recv())
        block = r.gp[i, y].astype(F32)
        for e in range(1, Y):
            block = block + r.gy[i, e].astype(F32)

        @pl.when(i < Z)
        def _():
            r.gz[i] = block.astype(BF16)
            z2(i).start()

        @pl.when(i == Z)
        def _():
            r.own[...] = block

    r.sum[...] = jnp.zeros_like(r.sum)

    def stage6(i):
        @pl.when(i < Z)
        def _():
            z2(i).wait_recv()
            r.sum[...] += r.gr[i].astype(F32)

    def drain_last():
        def one(i):
            z1(i).wait_send()
            z2(i).wait_send()

        loop(1, Z, one)

        def more(i):
            loop(1, Y, lambda e: y1(i, e).wait_send())
            loop(1, Y, lambda e: y2(i, e).wait_send())
            loop(1, X, lambda d: xx(i, d).wait_send())
            loop(0, X, lambda d: cc(i, d).wait_send())

        loop(1, Z + 1, more)

    stages = (
        (14, stage6),
        (11, stage5),
        (8, stage4),
        (6, stage3),
        (3, stage2),
        (0, stage1),
    )
    loop(1, Z + 1, stage0)

    def tick(k):
        for late, stage in stages:

            @pl.when((k - late >= 1) & (k - late <= Z))
            def _(late=late, stage=stage):
                stage(k - late)

    loop(1, Z + 1 + stages[0][0], tick)
    result[...] = r.sum[...] + r.own[...]

    drain_front()
    drain_middle()
    drain_last()


def whole(n, hidden, queries, keys, weight, readout, base, labels, rows):
    Z, Y, X, PP = n.Z, n.Y, n.X, n.P
    feat = hidden.shape[1] // PP
    qw = queries.shape[1] // Z
    kv = keys.shape[1]
    cand = readout.shape[1]
    chunk = Y * TOK
    dma = pltpu.SemaphoreType.DMA
    vmem = pltpu.VMEM
    scratch = dict(
        weight=vmem((feat, kv), BF16),
        readout=vmem((qw, cand), BF16),
        cols=vmem((PP, TOK, feat), BF16),
        qz=vmem((Z, TOK, qw), BF16),
        kz=vmem((n.S, TOK, HD), BF16),
        vz=vmem((n.S, TOK, HD), BF16),
        part=vmem((Z + 1, PP * TOK, HD), BF16),
        pair=vmem((Z + 1, X * TOK, HD), BF16),
        both=vmem((Z + 1, X * TOK, HD), BF16),
        xin=vmem((Z + 1, X, TOK, HD), BF16),
        val=vmem((Z + 1, TOK, HD), BF16),
        raw=vmem((Z * chunk, qw), F32),
        vt=vmem((Z, HD, chunk), BF16),
        out=vmem((HD, qw), F32),
        kept=vmem((Z * (Z + 1) // 2, chunk, qw), BF16),
        inverse=vmem((Z, 8, qw), F32),
        share=vmem((Z, TOK, cand), BF16),
        arrived=vmem((Z, TOK, cand), BF16),
        slopes=vmem((Z, TOK, cand), BF16),
        d_rows=vmem((HD, qw), BF16),
        total=vmem((Z, HD, chunk), F32),
        grads=vmem((Z + 1, Y, TOK, HD), BF16),
        ya=vmem((Z + 1, Y, TOK, HD), BF16),
        dz=vmem((Z + 1, TOK, HD), BF16),
        dv=vmem((PP, TOK, kv), BF16),
        gp=vmem((Z + 1, Y, rows, feat), BF16),
        gy=vmem((Z + 1, Y, rows, feat), BF16),
        gz=vmem((Z, rows, feat), BF16),
        gr=vmem((Z, rows, feat), BF16),
        sum=vmem((rows, feat), F32),
        own=vmem((rows, feat), F32),
        loc=dma((7,)),
    )
    for name in ("h",):
        scratch |= {name + "s": dma((PP,)), name + "r": dma((PP,))}
    for name in ("k", "q", "v", "l", "s", "z1", "z2"):
        scratch |= {name + "s": dma((Z,)), name + "r": dma((Z,))}
    scratch |= {"cs": dma((Z + 1,)), "cr": dma((Z + 1,))}
    for name in ("ky", "vy", "y1", "y2"):
        scratch |= {name + "s": dma((Z + 1, Y)), name + "r": dma((Z + 1, Y))}
    for name in ("x", "x2", "c2"):
        scratch |= {name + "s": dma((Z + 1, X)), name + "r": dma((Z + 1, X))}
    return pl.pallas_call(
        functools.partial(whole_kernel, n, tuple(scratch)),
        out_shape=jax.ShapeDtypeStruct((rows, feat), F32),
        in_specs=[ANY, ANY, ANY, ANY, ANY, VMEM, VMEM],
        out_specs=VMEM,
        scratch_shapes=list(scratch.values()),
        compiler_params=pltpu.CompilerParams(
            collective_id=0, has_side_effects=True, vmem_limit_bytes=64 * 1024 * 1000
        ),
        name="whole",
    )(hidden, queries, keys, weight, readout, base, labels)


def local(queries, keys, hidden, value_weight, readout, base_logits, labels, hessian):
    n = sizes_of(lax.axis_size("seq"), lax.axis_size("dp"))
    total = whole(
        n,
        hidden[0],
        queries[0],
        keys[0],
        value_weight,
        readout,
        base_logits[0],
        labels,
        hessian.shape[0],
    )
    estimate = total * total / (n.S * TOK * n.P)
    return estimate, beta_two * hessian + (1.0 - beta_two) * estimate


def solution(mesh):
    placed = (
        P("dp", "seq", None),
        P("dp", "seq", None),
        P("dp", "seq", None),
        P("dp", None),
        P(),
        P("dp", "seq", None),
        P("dp", "seq"),
        P("seq", "dp"),
    )
    return jax.shard_map(
        local,
        mesh=mesh,
        in_specs=placed,
        out_specs=(P("seq", "dp"), P("seq", "dp")),
        check_vma=False,
    )
```
